32 devices in a mesh: bus: 8 (over y, x, core), period: 4 (over z).
Axes of the slice: x: 2, y: 2, z: 4, core: 2. Of those that a mesh axis runs over, the one named last changes fastest.
Arguments:
- deviation: bfloat16 [128, 256, 128], P('bus', 'period'), may hold values from -6 to 6
- loading: bfloat16 [128, 256, 128], P('bus', 'period'), may hold values from 0.5 to 2
- jacobian: bfloat16 [128, 128, 128], P('bus'), may hold values from -0.5 to 0.5
- tie_source: int32 [128, 16], P('bus'), may hold values from 0 to 127
- tie_target: int32 [128, 16], P('bus'), may hold values from 0 to 127
- tie_admittance: float32 [128, 16], P('bus'), may hold values from 0.5 to 2
- condense: bfloat16 [128, 128, 512], P('bus'), may hold values from -0.046875 to 0.046875
- section_gain: bfloat16 [4, 64, 512, 512], P('period', 'bus'), may hold values from -0.0625 to 0.0625
- retention: float32 [4, 64, 512], P('period', 'bus'), may hold values from 0 to 1
Outputs:
- mismatch: bfloat16 [128, 256, 128], P('bus', 'period')
- section_states: float32 [4, 64, 512], P('period', 'bus')
The draws below stay inside these ranges and needn't reach their ends.
All inputs are finite; a program needn't handle non-finite values.
Results may differ from the reference program's by a relative error of at most 0.013.
Values may be sent and summed in bfloat16 or wider, within the bound.
No kernel may reach another device: no remote copies, remote signals or barrier semaphores. Data moves between devices by JAX's collectives and lax.ppermute only.
A program may use at most 64 MiB of HBM per device.

```python
import math
import jax
import jax.numpy as jnp
from jax import lax

S = 128
M = 512
EDGES = 16
NB = 128
PER_DEV = 64
GROUPS = 4
PERIODS = 256


def draw_retention(key, part):
    key_slow, key_rate, key_fast, key_rough, key_spots, key_cut = jax.random.split(key, 6)
    slow_share = 0.5
    slow_flag = jax.random.uniform(key_slow, (M,), jnp.float32) < slow_share
    slow_rate = jnp.exp(jax.random.uniform(key_rate, (M,), jnp.float32, jnp.log(0.02), jnp.log(0.5))) / PERIODS
    fast_rate = jnp.exp(jax.random.uniform(key_fast, (M,), jnp.float32, jnp.log(1.0 / 50.0), jnp.log(1.0 / 30.0)))
    nominal_rate = jnp.where(slow_flag, slow_rate, fast_rate)
    coarse_noise = jnp.exp(jax.random.uniform(key_rough, (PERIODS, M), jnp.float32, jnp.log(0.5), jnp.log(2.0)))
    chosen_locations = jax.random.randint(key_spots, (2,), 0, PERIODS)
    location_list = jnp.arange(PERIODS, dtype=jnp.int32)
    surge_struck = jnp.any(location_list[:, None] == chosen_locations[None, :], axis=1)
    threshold_split = jax.random.uniform(key_cut, (PERIODS, M), jnp.float32, 0.6, 0.8)
    surge_event = jnp.where(surge_struck[:, None] & slow_flag[None, :], threshold_split, 1.0)
    value_entries = jnp.exp(-nominal_rate[None, :] * coarse_noise) * surge_event
    return value_entries.reshape(GROUPS, PER_DEV, M)


def with_ends(result, rng, least, high):
    place = [jax.random.randint(jax.random.fold_in(rng, axis), (), 0, length) for axis, length in enumerate(result.shape)]
    longest = result.shape.index(max(result.shape))
    beside = place[:longest] + [(place[longest] + 1) % result.shape[longest]] + place[longest + 1:]
    return result.at[tuple(place)].set(least).at[tuple(beside)].set(high)


def level_of(rng, dims, pieces, least, high):
    loudness = 1.0
    for dim, shards_of in pieces:
        draws = jax.random.uniform(jax.random.fold_in(jax.random.fold_in(rng, 6), dim), (shards_of,), jnp.float32, least / len(pieces), high / len(pieces))
        loudness = loudness * jnp.repeat(jnp.exp(draws), dims[dim] // shards_of).reshape((-1,) + (1,) * (len(dims) - 1 - dim))
    return loudness


def bell_draw(stream_key, dims, scale, reach, shards=(), kind=jnp.bfloat16):
    result = jax.random.normal(stream_key, dims, jnp.float32) * scale
    if len(shards) > 0:
        result = level_of(stream_key, dims, shards, -0.22, 0.18) * result
    return jnp.clip(result, min=-reach, max=reach).astype(kind)


def setup_inputs(seed: int = 0) -> dict:
    key_list = jax.random.split(jax.random.key(seed), 10)
    deviation = bell_draw(key_list[0], (NB, PERIODS, S), 1.0, 6.0, ((0, 8), (1, 4)))
    loading = jnp.clip(jnp.exp(math.log(2.0) - 1.3862944 * jax.random.uniform(key_list[1], (NB, PERIODS, S), jnp.float32) ** level_of(key_list[1], (NB, PERIODS, S), ((0, 8), (1, 4)), -0.2, 0.2)), 0.5, 2.0).astype(jnp.bfloat16)
    jacobian = bell_draw(key_list[2], (NB, S, S), S ** -0.5, 0.5, ((0, 8),))
    tie_source = with_ends(jax.random.randint(key_list[3], (NB, EDGES), 0, S), jax.random.fold_in(key_list[3], 1), 0, S - 1).astype(jnp.int32)
    tie_target = with_ends(jax.random.randint(key_list[4], (NB, EDGES), 0, S), jax.random.fold_in(key_list[4], 1), 0, S - 1).astype(jnp.int32)
    tie_admittance = jnp.clip(jnp.exp(math.log(2.0) - 1.3862944 * jax.random.uniform(key_list[5], (NB, EDGES), jnp.float32) ** level_of(key_list[5], (NB, EDGES), ((0, 8),), -0.2, 0.2)), 0.5, 2.0)
    condense = bell_draw(key_list[6], (NB, S, M), (NB * S) ** -0.5, 0.046875, ((0, 8),))
    section_gain = bell_draw(key_list[7], (GROUPS, PER_DEV, M, M), (M * 16) ** -0.5, 0.0625, ((0, 4), (1, 8)))
    retention = draw_retention(jax.random.fold_in(key_list[9], 71), 0)
    return dict(deviation=deviation, loading=loading, jacobian=jacobian, tie_source=tie_source, tie_target=tie_target, tie_admittance=tie_admittance, condense=condense, section_gain=section_gain, retention=retention)


def reference(deviation, loading, jacobian, tie_source, tie_target, tie_admittance, condense, section_gain, retention):
    highest = lax.Precision.HIGHEST
    scaled = (deviation.astype(jnp.float32) * loading.astype(jnp.float32)).astype(jnp.bfloat16)
    scaled_full = scaled.astype(jnp.float32)
    network = jnp.einsum('btp,bpq->btq', scaled_full, jacobian.astype(jnp.float32), precision=highest)
    columns = jnp.arange(S, dtype=jnp.int32)
    source_hot = (tie_source[:, :, None] == columns[None, None, :]).astype(jnp.float32)
    target_hot = (tie_target[:, :, None] == columns[None, None, :]).astype(jnp.float32)
    next_block = jnp.concatenate([scaled_full[1:], jnp.zeros_like(scaled_full[:1])], axis=0)
    at_target = jnp.einsum('btq,beq->bte', next_block, target_hot, precision=highest)
    at_source = jnp.einsum('btq,beq->bte', scaled_full, source_hot, precision=highest)
    edge_flow = tie_admittance[:, None, :] * (at_target - at_source)
    own_terms = jnp.einsum('bte,beq->btq', edge_flow, source_hot, precision=highest)
    handed = -jnp.einsum('bte,beq->btq', edge_flow, target_hot, precision=highest)
    received = jnp.concatenate([jnp.zeros_like(handed[:1]), handed[:-1]], axis=0)
    mismatch = (network + own_terms + received).astype(jnp.bfloat16)

    def add_block(total, inputs):
        mis_block, cond_block = inputs
        return total + jnp.dot(mis_block, cond_block, preferred_element_type=jnp.float32), None

    section_sum, _ = lax.scan(add_block, jnp.zeros((PERIODS, M), jnp.float32), (mismatch, condense))
    section_in = section_sum.astype(jnp.bfloat16)
    gains = section_gain.reshape(PERIODS, M, M)

    def push_one(inputs):
        return jnp.dot(inputs[0][None, :], inputs[1], preferred_element_type=jnp.float32)[0]

    pushed = lax.map(push_one, (section_in, gains))
    keeps = retention.reshape(PERIODS, M)

    def advance(carried, inputs):
        retain, pushed_now = inputs
        section_now = retain * carried + pushed_now
        return section_now, section_now

    _, states = lax.scan(advance, jnp.zeros((M,), jnp.float32), (keeps, pushed))
    return mismatch, states.reshape(GROUPS, PER_DEV, M)
```

```python
import jax
import jax.numpy as jnp
from jax import lax
from jax.experimental import pallas as pl
from jax.experimental.pallas import tpu as pltpu
from jax.sharding import PartitionSpec as P

F32, BF16, I32 = jnp.float32, jnp.bfloat16, jnp.int32
VM = pl.BlockSpec(memory_space=pltpu.VMEM)
TIE_ROWS = 16
PARAMS = pltpu.CompilerParams(vmem_limit_bytes=48 * 1024 * 1024)


def dot(a, b):
    return jnp.dot(a, b, preferred_element_type=F32)


def dot_t(a, b):
    return lax.dot_general(a, b, (((1,), (1,)), ((), ())), preferred_element_type=F32)


def product(deviation, loading):
    return (deviation.astype(F32) * loading.astype(F32)).astype(BF16)


def hot_columns(index_row, width):
    rows = lax.broadcasted_iota(I32, (width, index_row.shape[1]), 0)
    return (rows == index_row).astype(F32).astype(BF16)


def halves(flow, edges):
    upper = flow.astype(BF16).astype(F32)
    lane = lax.broadcasted_iota(I32, flow.shape, 1)
    return jnp.where(lane % (2 * edges) < edges, upper, flow - upper).astype(BF16)


def row_chunks(total, size, body):
    if total <= size:
        body(pl.ds(0, total))
        return

    @pl.loop(0, total // size)
    def _(k):
        body(pl.ds(pl.multiple_of(k * size, size), size))


def halo_kernel(dev, load, src, tgt, adm, pair_out, chip_out, ties):
    blocks, rows, _ = dev.shape
    edges = src.shape[1]
    last = blocks - 1
    even = lax.axis_index("bus") % 2 == 0
    ties[...] = jnp.zeros_like(ties)
    a = adm[last : last + 1, :]
    high = a.astype(BF16).astype(F32)
    mid = (a - high).astype(BF16).astype(F32)
    ties[0:1, 0:edges] = src[last : last + 1, :].astype(F32)
    ties[1:2, 0:edges] = tgt[last : last + 1, :].astype(F32)
    ties[2:3, 0:edges] = high
    ties[3:4, 0:edges] = mid
    ties[4:5, 0:edges] = a - high - mid
    packed = ties[...].astype(BF16)

    @pl.when(even)
    def _():
        pair_out[0:rows, :] = product(dev[last], load[last])
        chip_out[0:rows, :] = product(dev[0], load[0])

    @pl.when(jnp.logical_not(even))
    def _():
        pair_out[0:rows, :] = product(dev[0], load[0])
        chip_out[0:rows, :] = product(dev[last], load[last])

    pair_out[rows : rows + TIE_ROWS, :] = packed
    chip_out[rows : rows + TIE_ROWS, :] = packed


def inner_kernel(dev, load, jac, src, tgt, adm, cond, mis, ends, part):
    blocks, total, width = dev.shape
    edges = src.shape[1]
    src4 = jnp.concatenate([src[...]] * 4, axis=1)
    tgt4 = jnp.concatenate([tgt[...]] * 4, axis=1)
    adm4 = jnp.concatenate([adm[...]] * 4, axis=1)
    low = lax.broadcasted_iota(I32, (1, 4 * edges), 1) < 2 * edges
    hots = []
    for b in range(blocks):
        before = tgt4[b - 1 : b] if b else jnp.full((1, 4 * edges), -1, I32)
        mine = src4[b : b + 1]
        hots.append(hot_columns(jnp.where(low, *((before, mine) if b % 2 else (mine, before))), width))

    def body(here):
        scaled = [product(dev[b, here, :], load[b, here, :]) for b in range(blocks)]
        picked = [dot(scaled[b], hots[b]) for b in range(blocks)]
        previous = None
        row = []
        for b in range(blocks):
            after = picked[b + 1] if b + 1 < blocks else 0.0
            flow = adm4[b : b + 1] * (after - picked[b])
            received = 0.0 if previous is None else -previous
            flows = halves(jnp.where(low, *((received, flow) if b % 2 else (flow, received))), edges)
            previous = flow
            whole = dot(scaled[b], jac[b]) + dot_t(flows, hots[b])
            if b == 0:
                ends[0, here, :] = whole
            elif b == blocks - 1:
                ends[1, here, :] = whole
            else:
                rounded = whole.astype(BF16)
                mis[b, here, :] = rounded
                row.append((b, rounded))
        sums = 0.0
        for k in range(0, len(row), 2):
            pair = row[k : k + 2]
            left = jnp.concatenate([value for _, value in pair], axis=1)
            first = pair[0][0]
            right = cond[first : first + len(pair)].reshape(len(pair) * width, cond.shape[2])
            sums = sums + dot(left, right)
        part[here, :] = sums

    row_chunks(total, 64, body)


def ends_kernel(dev, load, src, tgt, adm, cond, pair_in, chip_in, ends, part, mis, out):
    blocks, total, width = dev.shape
    edges = src.shape[1]
    last = blocks - 1
    place, count = lax.axis_index("bus"), lax.axis_size("bus")
    even = place % 2 == 0
    ties = jnp.where(even, chip_in[total : total + TIE_ROWS, :].astype(F32), pair_in[total : total + TIE_ROWS, :].astype(F32))

    def twice(row):
        return jnp.concatenate([row[:, 0:edges]] * 2, axis=1)

    src_before = hot_columns(twice(ties[0:1]).astype(I32), width)
    tgt_before = hot_columns(twice(ties[1:2]).astype(I32), width)
    adm_before = twice(ties[2:3] + ties[3:4] + ties[4:5])
    adm_before = jnp.where(place == 0, 0.0, adm_before)
    src_last = hot_columns(twice(src[last : last + 1]), width)
    tgt_last = hot_columns(twice(tgt[last : last + 1]), width)
    adm_last = jnp.where(place == count - 1, 0.0, twice(adm[last : last + 1]))
    right = jnp.concatenate([cond[0], cond[last]], axis=0)

    def body(here):
        pair_rows, chip_rows = pair_in[here, :].astype(F32), chip_in[here, :].astype(F32)
        following = jnp.where(even, pair_rows, chip_rows).astype(BF16)
        leading = jnp.where(even, chip_rows, pair_rows).astype(BF16)
        first = product(dev[0, here, :], load[0, here, :])
        flow_out = adm_last * dot(following, tgt_last)
        flow_in = adm_before * (dot(first, tgt_before) - dot(leading, src_before))
        low = (ends[0, here, :] - dot_t(halves(flow_in, edges), tgt_before)).astype(BF16)
        high = (ends[1, here, :] + dot_t(halves(flow_out, edges), src_last)).astype(BF16)
        mis[0, here, :] = low
        mis[1, here, :] = high
        sums = part[here, :] + dot(jnp.concatenate([low, high], axis=1), right)
        out[here, :] = sums.astype(BF16)

    row_chunks(total, 64, body)


def push_kernel(parts, gain, keep, inner, outer, states, running, sent, mis, sems):
    last = inner.shape[0] - 1
    copies_out = [
        pltpu.make_async_copy(inner.at[pl.ds(1, last - 1)], mis.at[pl.ds(1, last - 1)], sems.at[0]),
        pltpu.make_async_copy(outer.at[0], mis.at[0], sems.at[1]),
        pltpu.make_async_copy(outer.at[1], mis.at[last], sems.at[2]),
    ]
    for copy in copies_out:
        copy.start()
    count, rows, width = parts.shape
    copies = sent.shape[0]

    def add(k, total):
        return total + parts[k].astype(F32)

    section_in = lax.fori_loop(0, count, add, jnp.zeros((rows, width), F32), unroll=8).astype(BF16)
    line = lax.broadcasted_iota(I32, (rows, width), 0)
    pushed = jnp.zeros((rows, width), F32)
    for r in range(rows):
        pushed = jnp.where(line == r, dot(section_in, gain[r]), pushed)
    rate, state = keep[...], pushed
    shift = 1
    while shift < rows:
        reached = line >= shift
        state = state + jnp.where(reached, rate * pltpu.roll(state, shift, 0), 0.0)
        rate = rate * jnp.where(reached, pltpu.roll(rate, shift, 0), 1.0)
        shift *= 2
    states[...] = state
    running[...] = rate
    tiles = width // 128
    lines = [rate[rows - 1 : rows, 128 * k : 128 * k + 128] for k in range(tiles)]
    lines += [state[rows - 1 : rows, 128 * k : 128 * k + 128] for k in range(tiles)]
    both = jnp.concatenate(lines, axis=0)
    for k in range(copies):
        sent[k] = both
    for copy in copies_out:
        copy.wait()


def enter_kernel(spans, states, running, out):
    tiles = spans.shape[1] // 2
    place = lax.axis_index("period") * lax.axis_size("bus") + lax.axis_index("bus")

    def step(k, entering):
        return spans[k, 0:tiles] * entering + spans[k, tiles : 2 * tiles]

    entering = lax.fori_loop(0, place, step, jnp.zeros((tiles, 128), F32))
    flat = jnp.concatenate([entering[k : k + 1] for k in range(tiles)], axis=1)
    out[...] = states[...] + running[...] * flat


def call(kernel, shapes, inputs, scratch=(), specs=None):
    single = not isinstance(shapes, (list, tuple))
    return pl.pallas_call(
        kernel,
        out_shape=shapes,
        in_specs=[VM] * len(inputs),
        out_specs=specs or (VM if single else [VM] * len(shapes)),
        scratch_shapes=list(scratch),
        compiler_params=PARAMS,
    )(*inputs)


def shards(deviation, loading, jacobian, tie_source, tie_target, tie_admittance, condense, section_gain, retention):
    blocks, total, width = deviation.shape
    states_width = condense.shape[2]
    count = lax.axis_size("bus")
    spans = count * lax.axis_size("period")
    rows = section_gain.shape[1]
    shape = jax.ShapeDtypeStruct

    payload = shape((total + TIE_ROWS, width), BF16)
    pair_out, chip_out = call(
        halo_kernel,
        [payload, payload],
        (deviation, loading, tie_source, tie_target, tie_admittance),
        [pltpu.VMEM((TIE_ROWS, width), F32)],
    )
    pairs = [(k, k ^ 1) for k in range(count)]
    chips = [(k, (k + 1) % count if k % 2 else (k - 1) % count) for k in range(count)]
    pair_in = lax.ppermute(pair_out, "bus", pairs)
    chip_in = lax.ppermute(chip_out, "bus", chips)
    inner, ends, part = call(
        inner_kernel,
        [shape((blocks, total, width), BF16), shape((2, total, width), F32), shape((total, states_width), F32)],
        (deviation, loading, jacobian, tie_source, tie_target, tie_admittance, condense),
    )
    outer, sums = call(
        ends_kernel,
        [shape((2, total, width), BF16), shape((total, states_width), BF16)],
        (deviation, loading, tie_source, tie_target, tie_admittance, condense, pair_in, chip_in, ends, part),
    )
    parts = lax.all_to_all(sums.reshape(count, rows, states_width), "bus", 0, 0, tiled=True)
    tiles = 2 * states_width // 128
    states, running, sent, mismatch = call(
        push_kernel,
        [
            shape((rows, states_width), F32),
            shape((rows, states_width), F32),
            shape((spans, tiles, 128), F32),
            shape((blocks, total, width), BF16),
        ],
        (parts, section_gain[0], retention[0], inner, outer),
        [pltpu.SemaphoreType.DMA((3,))],
        [VM, VM, VM, pl.BlockSpec(memory_space=pl.ANY)],
    )
    everything = lax.all_to_all(sent, ("period", "bus"), 0, 0, tiled=True)
    out = call(enter_kernel, shape((rows, states_width), F32), (everything, states, running))
    return (mismatch, out[None])


def solution(mesh):
    placed = (
        P("bus", "period", None),
        P("bus", "period", None),
        P("bus", None, None),
        P("bus", None),
        P("bus", None),
        P("bus", None),
        P("bus", None, None),
        P("period", "bus", None, None),
        P("period", "bus", None),
    )
    return jax.shard_map(
        shards,
        mesh=mesh,
        in_specs=placed,
        out_specs=(P("bus", "period", None), P("period", "bus", None)),
        check_vma=False,
    )
```

```python
import jax
import jax.numpy as jnp
from jax import lax
from jax.experimental import pallas as pl
from jax.experimental.pallas import tpu as pltpu
from jax.sharding import PartitionSpec as P

F32, BF16, I32 = jnp.float32, jnp.bfloat16, jnp.int32
VM = pl.BlockSpec(memory_space=pltpu.VMEM)
TIE_ROWS = 16
PARAMS = pltpu.CompilerParams(vmem_limit_bytes=16 * 1024 * 1024)
HBM = pl.BlockSpec(memory_space=pltpu.HBM)


def dot(a, b):
    return jnp.dot(a, b, preferred_element_type=F32)


def dot_t(a, b):
    return lax.dot_general(a, b, (((1,), (1,)), ((), ())), preferred_element_type=F32)


def product(deviation, loading):
    return (deviation.astype(F32) * loading.astype(F32)).astype(BF16)


def hot_columns(index_row, width):
    rows = lax.broadcasted_iota(I32, (width, index_row.shape[1]), 0)
    return (rows == index_row).astype(F32).astype(BF16)


def halves(flow, edges):
    upper = flow.astype(BF16).astype(F32)
    lane = lax.broadcasted_iota(I32, flow.shape, 1)
    return jnp.where(lane % (2 * edges) < edges, upper, flow - upper).astype(BF16)


def row_chunks(total, size, body):
    if total <= size:
        body(pl.ds(0, total))
        return

    @pl.loop(0, total // size)
    def _(k):
        body(pl.ds(pl.multiple_of(k * size, size), size))


def halo_kernel(dev_hbm, load_hbm, src_hbm, tgt_hbm, adm_hbm, pair_out, chip_out, dev, load, src, tgt, adm, ties, sems):
    last = dev_hbm.shape[0] - 1
    rows = dev.shape[1]
    edges = src.shape[1]
    fetches = [
        pltpu.make_async_copy(source, target, sems.at[k])
        for k, (source, target) in enumerate(
            [
                (dev_hbm.at[0], dev.at[0]),
                (dev_hbm.at[last], dev.at[1]),
                (load_hbm.at[0], load.at[0]),
                (load_hbm.at[last], load.at[1]),
                (src_hbm, src),
                (tgt_hbm, tgt),
                (adm_hbm, adm),
            ]
        )
    ]
    for fetch in fetches:
        fetch.start()
    even = lax.axis_index("bus") % 2 == 0
    ties[...] = jnp.zeros_like(ties)
    for fetch in fetches:
        fetch.wait()
    a = adm[last : last + 1, :]
    high = a.astype(BF16).astype(F32)
    mid = (a - high).astype(BF16).astype(F32)
    ties[0:1, 0:edges] = src[last : last + 1, :].astype(F32)
    ties[1:2, 0:edges] = tgt[last : last + 1, :].astype(F32)
    ties[2:3, 0:edges] = high
    ties[3:4, 0:edges] = mid
    ties[4:5, 0:edges] = a - high - mid
    packed = ties[...].astype(BF16)

    first, final = product(dev[0], load[0]).astype(F32), product(dev[1], load[1]).astype(F32)
    pair_out[0:rows, :] = jnp.where(even, final, first).astype(BF16)
    chip_out[0:rows, :] = jnp.where(even, first, final).astype(BF16)
    pair_out[rows : rows + TIE_ROWS, :] = packed
    chip_out[rows : rows + TIE_ROWS, :] = packed


def inner_kernel(dev, load, jac, src, tgt, adm, cond, mis, ends, part):
    blocks, total, width = dev.shape
    edges = src.shape[1]
    src4 = jnp.concatenate([src[...]] * 4, axis=1)
    tgt4 = jnp.concatenate([tgt[...]] * 4, axis=1)
    adm4 = jnp.concatenate([adm[...]] * 4, axis=1)
    low = lax.broadcasted_iota(I32, (1, 4 * edges), 1) < 2 * edges
    hots = []
    for b in range(blocks):
        before = tgt4[b - 1 : b] if b else jnp.full((1, 4 * edges), -1, I32)
        mine = src4[b : b + 1]
        hots.append(hot_columns(jnp.where(low, *((before, mine) if b % 2 else (mine, before))), width))

    def body(here):
        scaled = [product(dev[b, here, :], load[b, here, :]) for b in range(blocks)]
        picked = [dot(scaled[b], hots[b]) for b in range(blocks)]
        previous = None
        row = []
        for b in range(blocks):
            after = picked[b + 1] if b + 1 < blocks else 0.0
            flow = adm4[b : b + 1] * (after - picked[b])
            received = 0.0 if previous is None else -previous
            flows = halves(jnp.where(low, *((received, flow) if b % 2 else (flow, received))), edges)
            previous = flow
            whole = dot(scaled[b], jac[b]) + dot_t(flows, hots[b])
            if b == 0:
                ends[0, here, :] = whole
            elif b == blocks - 1:
                ends[1, here, :] = whole
            else:
                rounded = whole.astype(BF16)
                mis[b, here, :] = rounded
                row.append((b, rounded))
        sums = 0.0
        for k in range(0, len(row), 2):
            pair = row[k : k + 2]
            left = jnp.concatenate([value for _, value in pair], axis=1)
            first = pair[0][0]
            right = cond[first : first + len(pair)].reshape(len(pair) * width, cond.shape[2])
            sums = sums + dot(left, right)
        part[here, :] = sums

    row_chunks(total, 64, body)


def ends_kernel(dev, load, src, tgt, adm, cond, pair_in, chip_in, ends, part, mis, out):
    blocks, total, width = dev.shape
    edges = src.shape[1]
    last = blocks - 1
    place, count = lax.axis_index("bus"), lax.axis_size("bus")
    even = place % 2 == 0
    ties = jnp.where(even, chip_in[total : total + TIE_ROWS, :].astype(F32), pair_in[total : total + TIE_ROWS, :].astype(F32))

    def twice(row):
        return jnp.concatenate([row[:, 0:edges]] * 2, axis=1)

    src_before = hot_columns(twice(ties[0:1]).astype(I32), width)
    tgt_before = hot_columns(twice(ties[1:2]).astype(I32), width)
    adm_before = twice(ties[2:3] + ties[3:4] + ties[4:5])
    adm_before = jnp.where(place == 0, 0.0, adm_before)
    src_last = hot_columns(twice(src[last : last + 1]), width)
    tgt_last = hot_columns(twice(tgt[last : last + 1]), width)
    adm_last = jnp.where(place == count - 1, 0.0, twice(adm[last : last + 1]))
    right = jnp.concatenate([cond[0], cond[last]], axis=0)

    def body(here):
        pair_rows, chip_rows = pair_in[here, :].astype(F32), chip_in[here, :].astype(F32)
        following = jnp.where(even, pair_rows, chip_rows).astype(BF16)
        leading = jnp.where(even, chip_rows, pair_rows).astype(BF16)
        first = product(dev[0, here, :], load[0, here, :])
        flow_out = adm_last * dot(following, tgt_last)
        flow_in = adm_before * (dot(first, tgt_before) - dot(leading, src_before))
        low = (ends[0, here, :] - dot_t(halves(flow_in, edges), tgt_before)).astype(BF16)
        high = (ends[1, here, :] + dot_t(halves(flow_out, edges), src_last)).astype(BF16)
        mis[0, here, :] = low
        mis[1, here, :] = high
        sums = part[here, :] + dot(jnp.concatenate([low, high], axis=1), right)
        out[here, :] = sums.astype(BF16)

    row_chunks(total, 64, body)


def push_kernel(parts, gain, keep, inner, outer, states, running, sent, mis, sems):
    last = inner.shape[0] - 1
    copies_out = [
        pltpu.make_async_copy(inner.at[pl.ds(1, last - 1)], mis.at[pl.ds(1, last - 1)], sems.at[0]),
        pltpu.make_async_copy(outer.at[0], mis.at[0], sems.at[1]),
        pltpu.make_async_copy(outer.at[1], mis.at[last], sems.at[2]),
    ]
    for copy in copies_out:
        copy.start()
    count, rows, width = parts.shape
    copies = sent.shape[0]

    def add(k, total):
        return total + parts[k].astype(F32)

    section_in = lax.fori_loop(0, count, add, jnp.zeros((rows, width), F32), unroll=8).astype(BF16)
    line = lax.broadcasted_iota(I32, (rows, width), 0)
    pushed = jnp.zeros((rows, width), F32)
    for r in range(rows):
        pushed = jnp.where(line == r, dot(section_in, gain[r]), pushed)
    rate, state = keep[...], pushed
    shift = 1
    while shift < rows:
        reached = line >= shift
        state = state + jnp.where(reached, rate * pltpu.roll(state, shift, 0), 0.0)
        rate = rate * jnp.where(reached, pltpu.roll(rate, shift, 0), 1.0)
        shift *= 2
    states[...] = state
    running[...] = rate
    tiles = width // 128
    lines = [rate[rows - 1 : rows, 128 * k : 128 * k + 128] for k in range(tiles)]
    lines += [state[rows - 1 : rows, 128 * k : 128 * k + 128] for k in range(tiles)]
    both = jnp.concatenate(lines, axis=0)
    for k in range(copies):
        sent[k] = both
    for copy in copies_out:
        copy.wait()


def enter_kernel(spans, states, running, out):
    tiles = spans.shape[1] // 2
    place = lax.axis_index("period") * lax.axis_size("bus") + lax.axis_index("bus")

    def step(k, entering):
        return spans[k, 0:tiles] * entering + spans[k, tiles : 2 * tiles]

    entering = lax.fori_loop(0, place, step, jnp.zeros((tiles, 128), F32))
    flat = jnp.concatenate([entering[k : k + 1] for k in range(tiles)], axis=1)
    out[...] = states[...] + running[...] * flat


def call(kernel, shapes, inputs, cost, scratch=(), specs=None, ins=None):
    single = not isinstance(shapes, (list, tuple))
    return pl.pallas_call(
        kernel,
        out_shape=shapes,
        in_specs=ins or [VM] * len(inputs),
        out_specs=specs or (VM if single else [VM] * len(shapes)),
        scratch_shapes=list(scratch),
        compiler_params=PARAMS,
        cost_estimate=pl.CostEstimate(flops=int(cost * 1e9), transcendentals=0, bytes_accessed=int(cost * 3.0e6)),
    )(*inputs)


def shards(deviation, loading, jacobian, tie_source, tie_target, tie_admittance, condense, section_gain, retention):
    blocks, total, width = deviation.shape
    states_width, edges = condense.shape[2], tie_source.shape[1]
    count = lax.axis_size("bus")
    spans = count * lax.axis_size("period")
    rows = section_gain.shape[1]
    shape = jax.ShapeDtypeStruct

    payload = shape((total + TIE_ROWS, width), BF16)
    pair_out, chip_out = call(
        halo_kernel,
        [payload, payload],
        [pltpu.with_memory_space_constraint(x, pltpu.HBM) for x in (deviation, loading, tie_source, tie_target, tie_admittance)],
        10.0,
        [
            pltpu.VMEM((2, total, width), BF16),
            pltpu.VMEM((2, total, width), BF16),
            pltpu.VMEM((blocks, edges), I32),
            pltpu.VMEM((blocks, edges), I32),
            pltpu.VMEM((blocks, edges), F32),
            pltpu.VMEM((TIE_ROWS, width), F32),
            pltpu.SemaphoreType.DMA((7,)),
        ],
        ins=[HBM] * 5,
    )
    pairs = [(k, k ^ 1) for k in range(count)]
    chips = [(k, (k + 1) % count if k % 2 else (k - 1) % count) for k in range(count)]
    pair_in = lax.ppermute(pair_out, "bus", pairs)
    chip_in = lax.ppermute(chip_out, "bus", chips)
    inner, ends, part = call(
        inner_kernel,
        [shape((blocks, total, width), BF16), shape((2, total, width), F32), shape((total, states_width), F32)],
        (deviation, loading, jacobian, tie_source, tie_target, tie_admittance, condense),
        5.0,
    )
    outer, sums = call(
        ends_kernel,
        [shape((2, total, width), BF16), shape((total, states_width), BF16)],
        (deviation, loading, tie_source, tie_target, tie_admittance, condense, pair_in, chip_in, ends, part),
        1.0,
    )
    parts = lax.all_to_all(sums.reshape(count, rows, states_width), "bus", 0, 0, tiled=True)
    tiles = 2 * states_width // 128
    states, running, sent, mismatch = call(
        push_kernel,
        [
            shape((rows, states_width), F32),
            shape((rows, states_width), F32),
            shape((spans, tiles, 128), F32),
            shape((blocks, total, width), BF16),
        ],
        (parts, section_gain[0], retention[0], inner, outer),
        2.0,
        [pltpu.SemaphoreType.DMA((3,))],
        [VM, VM, VM, HBM],
    )
    everything = lax.all_to_all(sent, ("period", "bus"), 0, 0, tiled=True)
    out = call(enter_kernel, shape((rows, states_width), F32), (everything, states, running), 1.0)
    return (mismatch, out[None])


def solution(mesh):
    placed = (
        P("bus", "period", None),
        P("bus", "period", None),
        P("bus", None, None),
        P("bus", None),
        P("bus", None),
        P("bus", None),
        P("bus", None, None),
        P("period", "bus", None, None),
        P("period", "bus", None),
    )
    return jax.shard_map(
        shards,
        mesh=mesh,
        in_specs=placed,
        out_specs=(P("bus", "period", None), P("period", "bus", None)),
        check_vma=False,
    )
```

```python
import jax
import jax.numpy as jnp
from jax import lax
from jax.experimental import pallas as pl
from jax.experimental.pallas import tpu as pltpu
from jax.sharding import PartitionSpec as P

F32, BF16, I32 = jnp.float32, jnp.bfloat16, jnp.int32
VM = pl.BlockSpec(memory_space=pltpu.VMEM)
TIE_ROWS = 16
PARAMS = pltpu.CompilerParams(vmem_limit_bytes=16 * 1024 * 1024)
HBM = pl.BlockSpec(memory_space=pltpu.HBM)


def dot(a, b):
    return jnp.dot(a, b, preferred_element_type=F32)


def dot_t(a, b):
    return lax.dot_general(a, b, (((1,), (1,)), ((), ())), preferred_element_type=F32)


def product(deviation, loading):
    return (deviation.astype(F32) * loading.astype(F32)).astype(BF16)


def hot_columns(index_row, width):
    rows = lax.broadcasted_iota(I32, (width, index_row.shape[1]), 0)
    return (rows == index_row).astype(F32).astype(BF16)


def halves(flow, edges):
    upper = flow.astype(BF16).astype(F32)
    lane = lax.broadcasted_iota(I32, flow.shape, 1)
    return jnp.where(lane % (2 * edges) < edges, upper, flow - upper).astype(BF16)


def row_chunks(total, size, body):
    if total <= size:
        body(pl.ds(0, total))
        return

    @pl.loop(0, total // size)
    def _(k):
        body(pl.ds(pl.multiple_of(k * size, size), size))


def halo_kernel(dev_hbm, load_hbm, src_hbm, tgt_hbm, adm_hbm, pair_out, chip_out, dev, load, src, tgt, adm, ties, sems):
    last = dev_hbm.shape[0] - 1
    rows = dev.shape[1]
    edges = src.shape[1]
    fetches = [
        pltpu.make_async_copy(source, target, sems.at[k])
        for k, (source, target) in enumerate(
            [
                (dev_hbm.at[0], dev.at[0]),
                (dev_hbm.at[last], dev.at[1]),
                (load_hbm.at[0], load.at[0]),
                (load_hbm.at[last], load.at[1]),
                (src_hbm, src),
                (tgt_hbm, tgt),
                (adm_hbm, adm),
            ]
        )
    ]
    for fetch in fetches:
        fetch.start()
    even = lax.axis_index("bus") % 2 == 0
    ties[...] = jnp.zeros_like(ties)
    for fetch in fetches:
        fetch.wait()
    a = adm[last : last + 1, :]
    high = a.astype(BF16).astype(F32)
    mid = (a - high).astype(BF16).astype(F32)
    ties[0:1, 0:edges] = src[last : last + 1, :].astype(F32)
    ties[1:2, 0:edges] = tgt[last : last + 1, :].astype(F32)
    ties[2:3, 0:edges] = high
    ties[3:4, 0:edges] = mid
    ties[4:5, 0:edges] = a - high - mid
    packed = ties[...].astype(BF16)

    first, final = product(dev[0], load[0]).astype(F32), product(dev[1], load[1]).astype(F32)
    pair_out[0:rows, :] = jnp.where(even, final, first).astype(BF16)
    chip_out[0:rows, :] = jnp.where(even, first, final).astype(BF16)
    pair_out[rows : rows + TIE_ROWS, :] = packed
    chip_out[rows : rows + TIE_ROWS, :] = packed


def inner_kernel(dev, load, jac, src, tgt, adm, cond, mis, ends, part):
    blocks, total, width = dev.shape
    edges = src.shape[1]
    src4 = jnp.concatenate([src[...]] * 4, axis=1)
    tgt4 = jnp.concatenate([tgt[...]] * 4, axis=1)
    adm4 = jnp.concatenate([adm[...]] * 4, axis=1)
    low = lax.broadcasted_iota(I32, (1, 4 * edges), 1) < 2 * edges
    hots = []
    for b in range(blocks):
        before = tgt4[b - 1 : b] if b else jnp.full((1, 4 * edges), -1, I32)
        mine = src4[b : b + 1]
        hots.append(hot_columns(jnp.where(low, *((before, mine) if b % 2 else (mine, before))), width))

    def body(here):
        scaled = [product(dev[b, here, :], load[b, here, :]) for b in range(blocks)]
        picked = [dot(scaled[b], hots[b]) for b in range(blocks)]
        previous = None
        row = []
        for b in range(blocks):
            after = picked[b + 1] if b + 1 < blocks else 0.0
            flow = adm4[b : b + 1] * (after - picked[b])
            received = 0.0 if previous is None else -previous
            flows = halves(jnp.where(low, *((received, flow) if b % 2 else (flow, received))), edges)
            previous = flow
            whole = dot(scaled[b], jac[b]) + dot_t(flows, hots[b])
            if b == 0:
                ends[0, here, :] = whole
            elif b == blocks - 1:
                ends[1, here, :] = whole
            else:
                rounded = whole.astype(BF16)
                mis[b, here, :] = rounded
                row.append((b, rounded))
        sums = 0.0
        for k in range(0, len(row), 2):
            pair = row[k : k + 2]
            left = jnp.concatenate([value for _, value in pair], axis=1)
            first = pair[0][0]
            right = cond[first : first + len(pair)].reshape(len(pair) * width, cond.shape[2])
            sums = sums + dot(left, right)
        part[here, :] = sums

    row_chunks(total, 64, body)


def ends_kernel(dev, load, src, tgt, adm, cond, chip_in, pair_in, ends, part, mis, out):
    blocks, total, width = dev.shape
    edges = src.shape[1]
    last = blocks - 1
    place, count = lax.axis_index("bus"), lax.axis_size("bus")
    even = place % 2 == 0
    ties = jnp.where(even, chip_in[total : total + TIE_ROWS, :].astype(F32), pair_in[total : total + TIE_ROWS, :].astype(F32))

    def twice(row):
        return jnp.concatenate([row[:, 0:edges]] * 2, axis=1)

    src_before = hot_columns(twice(ties[0:1]).astype(I32), width)
    tgt_before = hot_columns(twice(ties[1:2]).astype(I32), width)
    adm_before = twice(ties[2:3] + ties[3:4] + ties[4:5])
    adm_before = jnp.where(place == 0, 0.0, adm_before)
    src_last = hot_columns(twice(src[last : last + 1]), width)
    tgt_last = hot_columns(twice(tgt[last : last + 1]), width)
    adm_last = jnp.where(place == count - 1, 0.0, twice(adm[last : last + 1]))
    right = jnp.concatenate([cond[0], cond[last]], axis=0)

    def body(here):
        pair_rows, chip_rows = pair_in[here, :].astype(F32), chip_in[here, :].astype(F32)
        following = jnp.where(even, pair_rows, chip_rows).astype(BF16)
        leading = jnp.where(even, chip_rows, pair_rows).astype(BF16)
        first = product(dev[0, here, :], load[0, here, :])
        flow_out = adm_last * dot(following, tgt_last)
        flow_in = adm_before * (dot(first, tgt_before) - dot(leading, src_before))
        low = (ends[0, here, :] - dot_t(halves(flow_in, edges), tgt_before)).astype(BF16)
        high = (ends[1, here, :] + dot_t(halves(flow_out, edges), src_last)).astype(BF16)
        mis[0, here, :] = low
        mis[1, here, :] = high
        sums = part[here, :] + dot(jnp.concatenate([low, high], axis=1), right)
        out[here, :] = sums.astype(BF16)

    row_chunks(total, 64, body)


def push_kernel(parts, gain, keep, inner, outer, states, running, sent, mis, sems):
    last = inner.shape[0] - 1
    copies_out = [
        pltpu.make_async_copy(inner.at[pl.ds(1, last - 1)], mis.at[pl.ds(1, last - 1)], sems.at[0]),
        pltpu.make_async_copy(outer.at[0], mis.at[0], sems.at[1]),
        pltpu.make_async_copy(outer.at[1], mis.at[last], sems.at[2]),
    ]
    for copy in copies_out:
        copy.start()
    count, rows, width = parts.shape
    copies = sent.shape[0]

    def add(k, total):
        return total + parts[k].astype(F32)

    section_in = lax.fori_loop(0, count, add, jnp.zeros((rows, width), F32), unroll=8).astype(BF16)
    line = lax.broadcasted_iota(I32, (rows, width), 0)
    pushed = jnp.zeros((rows, width), F32)
    for r in range(rows):
        pushed = jnp.where(line == r, dot(section_in, gain[r]), pushed)
    rate, state = keep[...], pushed
    shift = 1
    while shift < rows:
        reached = line >= shift
        state = state + jnp.where(reached, rate * pltpu.roll(state, shift, 0), 0.0)
        rate = rate * jnp.where(reached, pltpu.roll(rate, shift, 0), 1.0)
        shift *= 2
    states[...] = state
    running[...] = rate
    tiles = width // 128
    lines = [rate[rows - 1 : rows, 128 * k : 128 * k + 128] for k in range(tiles)]
    lines += [state[rows - 1 : rows, 128 * k : 128 * k + 128] for k in range(tiles)]
    both = jnp.concatenate(lines, axis=0)
    for k in range(copies):
        sent[k] = both
    for copy in copies_out:
        copy.wait()


def enter_kernel(spans, states, running, out):
    tiles = spans.shape[1] // 2
    place = lax.axis_index("period") * lax.axis_size("bus") + lax.axis_index("bus")

    def step(k, entering):
        return spans[k, 0:tiles] * entering + spans[k, tiles : 2 * tiles]

    entering = lax.fori_loop(0, place, step, jnp.zeros((tiles, 128), F32))
    flat = jnp.concatenate([entering[k : k + 1] for k in range(tiles)], axis=1)
    out[...] = states[...] + running[...] * flat


def call(kernel, shapes, inputs, cost, scratch=(), specs=None, ins=None):
    single = not isinstance(shapes, (list, tuple))
    return pl.pallas_call(
        kernel,
        out_shape=shapes,
        in_specs=ins or [VM] * len(inputs),
        out_specs=specs or (VM if single else [VM] * len(shapes)),
        scratch_shapes=list(scratch),
        compiler_params=PARAMS,
        cost_estimate=pl.CostEstimate(flops=int(cost * 1e9), transcendentals=0, bytes_accessed=int(cost * 3.0e6)),
    )(*inputs)


def shards(deviation, loading, jacobian, tie_source, tie_target, tie_admittance, condense, section_gain, retention):
    blocks, total, width = deviation.shape
    states_width, edges = condense.shape[2], tie_source.shape[1]
    count = lax.axis_size("bus")
    spans = count * lax.axis_size("period")
    rows = section_gain.shape[1]
    shape = jax.ShapeDtypeStruct

    payload = shape((total + TIE_ROWS, width), BF16)
    pair_out, chip_out = call(
        halo_kernel,
        [payload, payload],
        [pltpu.with_memory_space_constraint(x, pltpu.HBM) for x in (deviation, loading, tie_source, tie_target, tie_admittance)],
        10.0,
        [
            pltpu.VMEM((2, total, width), BF16),
            pltpu.VMEM((2, total, width), BF16),
            pltpu.VMEM((blocks, edges), I32),
            pltpu.VMEM((blocks, edges), I32),
            pltpu.VMEM((blocks, edges), F32),
            pltpu.VMEM((TIE_ROWS, width), F32),
            pltpu.SemaphoreType.DMA((7,)),
        ],
        ins=[HBM] * 5,
    )
    pairs = [(k, k ^ 1) for k in range(count)]
    chips = [(k, (k + 1) % count if k % 2 else (k - 1) % count) for k in range(count)]
    chip_in = lax.ppermute(chip_out, "bus", chips)
    pair_in = lax.ppermute(pair_out, "bus", pairs)
    inner, ends, part = call(
        inner_kernel,
        [shape((blocks, total, width), BF16), shape((2, total, width), F32), shape((total, states_width), F32)],
        (deviation, loading, jacobian, tie_source, tie_target, tie_admittance, condense),
        5.0,
    )
    outer, sums = call(
        ends_kernel,
        [shape((2, total, width), BF16), shape((total, states_width), BF16)],
        (deviation, loading, tie_source, tie_target, tie_admittance, condense, chip_in, pair_in, ends, part),
        1.0,
    )
    parts = lax.all_to_all(sums.reshape(count, rows, states_width), "bus", 0, 0, tiled=True)
    tiles = 2 * states_width // 128
    states, running, sent, mismatch = call(
        push_kernel,
        [
            shape((rows, states_width), F32),
            shape((rows, states_width), F32),
            shape((spans, tiles, 128), F32),
            shape((blocks, total, width), BF16),
        ],
        (parts, section_gain[0], retention[0], inner, outer),
        2.0,
        [pltpu.SemaphoreType.DMA((3,))],
        [VM, VM, VM, HBM],
    )
    everything = lax.all_to_all(sent, ("period", "bus"), 0, 0, tiled=True)
    out = call(enter_kernel, shape((rows, states_width), F32), (everything, states, running), 1.0)
    return (mismatch, out[None])


def solution(mesh):
    placed = (
        P("bus", "period", None),
        P("bus", "period", None),
        P("bus", None, None),
        P("bus", None),
        P("bus", None),
        P("bus", None),
        P("bus", None, None),
        P("period", "bus", None, None),
        P("period", "bus", None),
    )
    return jax.shard_map(
        shards,
        mesh=mesh,
        in_specs=placed,
        out_specs=(P("bus", "period", None), P("period", "bus", None)),
        check_vma=False,
    )
```

```python
import jax
import jax.numpy as jnp
from jax import lax
from jax.experimental import pallas as pl
from jax.experimental.pallas import tpu as pltpu
from jax.sharding import PartitionSpec as P

F32, BF16, I32 = jnp.float32, jnp.bfloat16, jnp.int32
VM = pl.BlockSpec(memory_space=pltpu.VMEM)
TIE_ROWS = 16
PARAMS = pltpu.CompilerParams(vmem_limit_bytes=16 * 1024 * 1024)
HBM = pl.BlockSpec(memory_space=pltpu.HBM)


def dot(a, b):
    return jnp.dot(a, b, preferred_element_type=F32)


def dot_t(a, b):
    return lax.dot_general(a, b, (((1,), (1,)), ((), ())), preferred_element_type=F32)


def product(deviation, loading):
    return (deviation.astype(F32) * loading.astype(F32)).astype(BF16)


def hot_columns(index_row, width):
    rows = lax.broadcasted_iota(I32, (width, index_row.shape[1]), 0)
    return (rows == index_row).astype(F32).astype(BF16)


def halves(flow, edges):
    upper = flow.astype(BF16).astype(F32)
    lane = lax.broadcasted_iota(I32, flow.shape, 1)
    return jnp.where(lane % (2 * edges) < edges, upper, flow - upper).astype(BF16)


def folded(row):
    return jnp.concatenate([row[:, 128 * k : 128 * k + 128] for k in range(row.shape[1] // 128)], axis=0)


def unfolded(rows):
    return jnp.concatenate([rows[k : k + 1] for k in range(rows.shape[0])], axis=1)


def row_chunks(total, size, body):
    if total <= size:
        body(pl.ds(0, total))
        return

    @pl.loop(0, total // size)
    def _(k):
        body(pl.ds(pl.multiple_of(k * size, size), size))


def halo_kernel(dev_hbm, load_hbm, src_hbm, tgt_hbm, adm_hbm, pair_out, chip_out, dev, load, src, tgt, adm, ties, sems):
    last = dev_hbm.shape[0] - 1
    rows = dev.shape[1]
    edges = src.shape[1]
    fetches = [
        pltpu.make_async_copy(source, target, sems.at[k])
        for k, (source, target) in enumerate(
            [
                (dev_hbm.at[0], dev.at[0]),
                (dev_hbm.at[last], dev.at[1]),
                (load_hbm.at[0], load.at[0]),
                (load_hbm.at[last], load.at[1]),
                (src_hbm, src),
                (tgt_hbm, tgt),
                (adm_hbm, adm),
            ]
        )
    ]
    for fetch in fetches:
        fetch.start()
    even = lax.axis_index("bus") % 2 == 0
    ties[...] = jnp.zeros_like(ties)
    for fetch in fetches:
        fetch.wait()
    a = adm[last : last + 1, :]
    high = a.astype(BF16).astype(F32)
    mid = (a - high).astype(BF16).astype(F32)
    ties[0:1, 0:edges] = src[last : last + 1, :].astype(F32)
    ties[1:2, 0:edges] = tgt[last : last + 1, :].astype(F32)
    ties[2:3, 0:edges] = high
    ties[3:4, 0:edges] = mid
    ties[4:5, 0:edges] = a - high - mid
    packed = ties[...].astype(BF16)

    first, final = product(dev[0], load[0]).astype(F32), product(dev[1], load[1]).astype(F32)
    pair_out[0:rows, :] = jnp.where(even, final, first).astype(BF16)
    chip_out[0:rows, :] = jnp.where(even, first, final).astype(BF16)
    pair_out[rows : rows + TIE_ROWS, :] = packed
    chip_out[rows : rows + TIE_ROWS, :] = packed


def inner_kernel(dev, load, jac, src, tgt, adm, cond, mis, ends, part):
    blocks, total, width = dev.shape
    edges = src.shape[1]
    src4 = jnp.concatenate([src[...]] * 4, axis=1)
    tgt4 = jnp.concatenate([tgt[...]] * 4, axis=1)
    adm4 = jnp.concatenate([adm[...]] * 4, axis=1)
    low = lax.broadcasted_iota(I32, (1, 4 * edges), 1) < 2 * edges
    hots = []
    for b in range(blocks):
        before = tgt4[b - 1 : b] if b else jnp.full((1, 4 * edges), -1, I32)
        mine = src4[b : b + 1]
        hots.append(hot_columns(jnp.where(low, *((before, mine) if b % 2 else (mine, before))), width))

    def body(here):
        scaled = [product(dev[b, here, :], load[b, here, :]) for b in range(blocks)]
        picked = [dot(scaled[b], hots[b]) for b in range(blocks)]
        previous = None
        row = []
        for b in range(blocks):
            after = picked[b + 1] if b + 1 < blocks else 0.0
            flow = adm4[b : b + 1] * (after - picked[b])
            received = 0.0 if previous is None else -previous
            flows = halves(jnp.where(low, *((received, flow) if b % 2 else (flow, received))), edges)
            previous = flow
            whole = dot(scaled[b], jac[b]) + dot_t(flows, hots[b])
            if b == 0:
                ends[0, here, :] = whole
            elif b == blocks - 1:
                ends[1, here, :] = whole
            else:
                rounded = whole.astype(BF16)
                mis[b, here, :] = rounded
                row.append((b, rounded))
        sums = 0.0
        for k in range(0, len(row), 2):
            pair = row[k : k + 2]
            left = jnp.concatenate([value for _, value in pair], axis=1)
            first = pair[0][0]
            right = cond[first : first + len(pair)].reshape(len(pair) * width, cond.shape[2])
            sums = sums + dot(left, right)
        part[here, :] = sums

    row_chunks(total, 64, body)


def ends_kernel(dev, load, src, tgt, adm, cond, chip_in, pair_in, ends, part, keep, mis, out):
    blocks, total, width = dev.shape
    edges = src.shape[1]
    last = blocks - 1
    place, count = lax.axis_index("bus"), lax.axis_size("bus")
    even = place % 2 == 0
    ties = jnp.where(even, chip_in[total : total + TIE_ROWS, :].astype(F32), pair_in[total : total + TIE_ROWS, :].astype(F32))

    def twice(row):
        return jnp.concatenate([row[:, 0:edges]] * 2, axis=1)

    src_before = hot_columns(twice(ties[0:1]).astype(I32), width)
    tgt_before = hot_columns(twice(ties[1:2]).astype(I32), width)
    adm_before = twice(ties[2:3] + ties[3:4] + ties[4:5])
    adm_before = jnp.where(place == 0, 0.0, adm_before)
    src_last = hot_columns(twice(src[last : last + 1]), width)
    tgt_last = hot_columns(twice(tgt[last : last + 1]), width)
    adm_last = jnp.where(place == count - 1, 0.0, twice(adm[last : last + 1]))
    right = jnp.concatenate([cond[0], cond[last]], axis=0)
    reach = cond.shape[2]
    rate = keep[...]
    while rate.shape[0] > 1:
        half = rate.shape[0] // 2
        rate = rate[0:half] * rate[half : 2 * half]
    rate = folded(rate)
    upper = rate.astype(BF16).astype(F32)
    rate = jnp.concatenate([upper, rate - upper], axis=0)
    size = rate.shape[0]
    for k in range(0, total, 2 * size):
        out[k : k + 2 * size, reach : reach + 128] = jnp.concatenate([rate, rate], axis=0).astype(BF16)

    def body(here):
        pair_rows, chip_rows = pair_in[here, :].astype(F32), chip_in[here, :].astype(F32)
        following = jnp.where(even, pair_rows, chip_rows).astype(BF16)
        leading = jnp.where(even, chip_rows, pair_rows).astype(BF16)
        first = product(dev[0, here, :], load[0, here, :])
        flow_out = adm_last * dot(following, tgt_last)
        flow_in = adm_before * (dot(first, tgt_before) - dot(leading, src_before))
        low = (ends[0, here, :] - dot_t(halves(flow_in, edges), tgt_before)).astype(BF16)
        high = (ends[1, here, :] + dot_t(halves(flow_out, edges), src_last)).astype(BF16)
        mis[0, here, :] = low
        mis[1, here, :] = high
        sums = part[here, :] + dot(jnp.concatenate([low, high], axis=1), right)
        out[here, 0:reach] = sums.astype(BF16)

    row_chunks(total, 64, body)


def push_kernel(parts, gain, keep, inner, outer, states, running, rates, sent, mis, sems):
    last = inner.shape[0] - 1
    copies_out = [
        pltpu.make_async_copy(inner.at[pl.ds(1, last - 1)], mis.at[pl.ds(1, last - 1)], sems.at[0]),
        pltpu.make_async_copy(outer.at[0], mis.at[0], sems.at[1]),
        pltpu.make_async_copy(outer.at[1], mis.at[last], sems.at[2]),
    ]
    for copy in copies_out:
        copy.start()
    count, rows, _ = parts.shape
    width = gain.shape[2]
    tiles = width // 128
    place, group = lax.axis_index("bus"), lax.axis_index("period")

    def add(k, total):
        return total + parts[k, :, 0:width].astype(F32)

    section_in = lax.fori_loop(0, count, add, jnp.zeros((rows, width), F32), unroll=8).astype(BF16)
    line = lax.broadcasted_iota(I32, (rows, width), 0)
    pushed = jnp.zeros((rows, width), F32)
    for r in range(rows):
        pushed = jnp.where(line == r, dot(section_in, gain[r]), pushed)
    rate, state = keep[...], pushed
    shift = 1
    while shift < rows:
        reached = line >= shift
        state = state + jnp.where(reached, rate * pltpu.roll(state, shift, 0), 0.0)
        rate = rate * jnp.where(reached, pltpu.roll(rate, shift, 0), 1.0)
        shift *= 2
    states[...] = state
    running[...] = rate

    def gather(k, carried):
        after, whole = carried
        both = parts[k, :, width : width + 128].astype(F32)
        span = both[0:tiles] + both[tiles : 2 * tiles]
        rates[k] = span
        return (after * jnp.where(k > place, span, 1.0), whole * span)

    ones = jnp.ones((tiles, 128), F32)
    after, whole = lax.fori_loop(0, count, gather, (ones, ones), unroll=8)
    upper = whole.astype(BF16).astype(F32)
    share = jnp.where(place % 2 == 0, upper, whole - upper)
    last_state = folded(state[rows - 1 : rows])
    here = jnp.concatenate([last_state, share], axis=0)
    beyond = jnp.concatenate([last_state * after, share], axis=0)
    for q in range(sent.shape[0] // count):
        value = jnp.where(group == q, here, beyond).astype(BF16)
        for k in range(count):
            sent[q * count + k] = value
    for copy in copies_out:
        copy.wait()


def enter_kernel(spans, rates, states, running, out):
    count, tiles, _ = rates.shape
    place, group = lax.axis_index("bus"), lax.axis_index("period")

    def add(k, total):
        return total + spans[k].astype(F32)

    entering = jnp.zeros((tiles, 128), F32)
    for q in range(spans.shape[0] // count - 1):
        first = q * count
        total = lax.fori_loop(first, first + count, add, jnp.zeros((2 * tiles, 128), F32), unroll=8)[0:tiles]
        pair = (spans[first].astype(F32) + spans[first + 1].astype(F32))[tiles : 2 * tiles]
        entering = jnp.where(q < group, pair * entering + total, entering)

    def step(k, entering):
        state = spans[group * count + k].astype(F32)[0:tiles]
        return jnp.where(k < place, rates[k] * entering + state, entering)

    entering = lax.fori_loop(0, count, step, entering, unroll=8)
    out[...] = states[...] + running[...] * unfolded(entering)


def call(kernel, shapes, inputs, cost, scratch=(), specs=None, ins=None):
    single = not isinstance(shapes, (list, tuple))
    return pl.pallas_call(
        kernel,
        out_shape=shapes,
        in_specs=ins or [VM] * len(inputs),
        out_specs=specs or (VM if single else [VM] * len(shapes)),
        scratch_shapes=list(scratch),
        compiler_params=PARAMS,
        cost_estimate=pl.CostEstimate(flops=int(cost * 1e9), transcendentals=0, bytes_accessed=int(cost * 3.0e6)),
    )(*inputs)


def shards(deviation, loading, jacobian, tie_source, tie_target, tie_admittance, condense, section_gain, retention):
    blocks, total, width = deviation.shape
    states_width, edges = condense.shape[2], tie_source.shape[1]
    count = lax.axis_size("bus")
    spans = count * lax.axis_size("period")
    rows = section_gain.shape[1]
    shape = jax.ShapeDtypeStruct

    payload = shape((total + TIE_ROWS, width), BF16)
    pair_out, chip_out = call(
        halo_kernel,
        [payload, payload],
        [pltpu.with_memory_space_constraint(x, pltpu.HBM) for x in (deviation, loading, tie_source, tie_target, tie_admittance)],
        10.0,
        [
            pltpu.VMEM((2, total, width), BF16),
            pltpu.VMEM((2, total, width), BF16),
            pltpu.VMEM((blocks, edges), I32),
            pltpu.VMEM((blocks, edges), I32),
            pltpu.VMEM((blocks, edges), F32),
            pltpu.VMEM((TIE_ROWS, width), F32),
            pltpu.SemaphoreType.DMA((7,)),
        ],
        ins=[HBM] * 5,
    )
    pairs = [(k, k ^ 1) for k in range(count)]
    groups = lax.axis_size("period")
    chips = []
    for k in range(count):
        partner = k + 1 if k % 2 else k - 1
        for g in range(groups):
            if 0 <= partner < count:
                chips.append((k * groups + g, partner * groups + g))
            else:
                chips.append((k * groups + g, k * groups + g ^ 1))
    chip_in = lax.ppermute(chip_out, ("bus", "period"), chips)
    pair_in = lax.ppermute(pair_out, "bus", pairs)
    inner, ends, part = call(
        inner_kernel,
        [shape((blocks, total, width), BF16), shape((2, total, width), F32), shape((total, states_width), F32)],
        (deviation, loading, jacobian, tie_source, tie_target, tie_admittance, condense),
        5.0,
    )
    outer, sums = call(
        ends_kernel,
        [shape((2, total, width), BF16), shape((total, states_width + 128), BF16)],
        (deviation, loading, tie_source, tie_target, tie_admittance, condense, chip_in, pair_in, ends, part, retention[0]),
        1.0,
    )
    parts = lax.all_to_all(sums.reshape(count, rows, states_width + 128), "bus", 0, 0, tiled=True)
    tiles = 2 * states_width // 128
    states, running, rates, sent, mismatch = call(
        push_kernel,
        [
            shape((rows, states_width), F32),
            shape((rows, states_width), F32),
            shape((count, tiles // 2, 128), F32),
            shape((spans, tiles, 128), BF16),
            shape((blocks, total, width), BF16),
        ],
        (parts, section_gain[0], retention[0], inner, outer),
        2.0,
        [pltpu.SemaphoreType.DMA((3,))],
        [VM, VM, VM, VM, HBM],
    )
    everything = lax.all_to_all(sent, ("period", "bus"), 0, 0, tiled=True)
    out = call(enter_kernel, shape((rows, states_width), F32), (everything, rates, states, running), 1.0)
    return (mismatch, out[None])


def solution(mesh):
    placed = (
        P("bus", "period", None),
        P("bus", "period", None),
        P("bus", None, None),
        P("bus", None),
        P("bus", None),
        P("bus", None),
        P("bus", None, None),
        P("period", "bus", None, None),
        P("period", "bus", None),
    )
    return jax.shard_map(
        shards,
        mesh=mesh,
        in_specs=placed,
        out_specs=(P("bus", "period", None), P("period", "bus", None)),
        check_vma=False,
    )
```

```python
import jax
import jax.numpy as jnp
from jax import lax
from jax.experimental import pallas as pl
from jax.experimental.pallas import tpu as pltpu
from jax.sharding import PartitionSpec as P

F32, BF16, I32 = jnp.float32, jnp.bfloat16, jnp.int32
VM = pl.BlockSpec(memory_space=pltpu.VMEM)
TIE_ROWS = 16
PARAMS = pltpu.CompilerParams(vmem_limit_bytes=16 * 1024 * 1024)
HBM = pl.BlockSpec(memory_space=pltpu.HBM)


def dot(a, b):
    return jnp.dot(a, b, preferred_element_type=F32)


def dot_t(a, b):
    return lax.dot_general(a, b, (((1,), (1,)), ((), ())), preferred_element_type=F32)


def product(deviation, loading):
    return (deviation.astype(F32) * loading.astype(F32)).astype(BF16)


def hot_columns(index_row, width):
    rows = lax.broadcasted_iota(I32, (width, index_row.shape[1]), 0)
    return (rows == index_row).astype(F32).astype(BF16)


def halves(flow, edges):
    upper = flow.astype(BF16).astype(F32)
    lane = lax.broadcasted_iota(I32, flow.shape, 1)
    return jnp.where(lane % (2 * edges) < edges, upper, flow - upper).astype(BF16)


def folded(row):
    return jnp.concatenate([row[:, 128 * k : 128 * k + 128] for k in range(row.shape[1] // 128)], axis=0)


def unfolded(rows):
    return jnp.concatenate([rows[k : k + 1] for k in range(rows.shape[0])], axis=1)


def row_chunks(total, size, body):
    if total <= size:
        body(pl.ds(0, total))
        return

    @pl.loop(0, total // size)
    def _(k):
        body(pl.ds(pl.multiple_of(k * size, size), size))


def halo_kernel(dev_hbm, load_hbm, src_hbm, tgt_hbm, adm_hbm, pair_out, chip_out, dev, load, src, tgt, adm, ties, sems):
    last = dev_hbm.shape[0] - 1
    rows = dev.shape[1]
    edges = src.shape[1]
    fetches = [
        pltpu.make_async_copy(source, target, sems.at[k])
        for k, (source, target) in enumerate(
            [
                (dev_hbm.at[0], dev.at[0]),
                (dev_hbm.at[last], dev.at[1]),
                (load_hbm.at[0], load.at[0]),
                (load_hbm.at[last], load.at[1]),
                (src_hbm, src),
                (tgt_hbm, tgt),
                (adm_hbm, adm),
            ]
        )
    ]
    for fetch in fetches:
        fetch.start()
    even = lax.axis_index("bus") % 2 == 0
    ties[...] = jnp.zeros_like(ties)
    for fetch in fetches:
        fetch.wait()
    a = adm[last : last + 1, :]
    high = a.astype(BF16).astype(F32)
    mid = (a - high).astype(BF16).astype(F32)
    ties[0:1, 0:edges] = src[last : last + 1, :].astype(F32)
    ties[1:2, 0:edges] = tgt[last : last + 1, :].astype(F32)
    ties[2:3, 0:edges] = high
    ties[3:4, 0:edges] = mid
    ties[4:5, 0:edges] = a - high - mid
    packed = ties[...].astype(BF16)

    first, final = product(dev[0], load[0]).astype(F32), product(dev[1], load[1]).astype(F32)
    pair_out[0:rows, :] = jnp.where(even, final, first).astype(BF16)
    chip_out[0:rows, :] = jnp.where(even, first, final).astype(BF16)
    pair_out[rows : rows + TIE_ROWS, :] = packed
    chip_out[rows : rows + TIE_ROWS, :] = packed


def inner_kernel(dev, load, jac, src, tgt, adm, cond, mis_hbm, ends, part, mis, sem):
    blocks, total, width = dev.shape
    edges = src.shape[1]
    src4 = jnp.concatenate([src[...]] * 4, axis=1)
    tgt4 = jnp.concatenate([tgt[...]] * 4, axis=1)
    adm4 = jnp.concatenate([adm[...]] * 4, axis=1)
    low = lax.broadcasted_iota(I32, (1, 4 * edges), 1) < 2 * edges
    hots = []
    for b in range(blocks):
        before = tgt4[b - 1 : b] if b else jnp.full((1, 4 * edges), -1, I32)
        mine = src4[b : b + 1]
        hots.append(hot_columns(jnp.where(low, *((before, mine) if b % 2 else (mine, before))), width))

    def body(here):
        scaled = [product(dev[b, here, :], load[b, here, :]) for b in range(blocks)]
        picked = [dot(scaled[b], hots[b]) for b in range(blocks)]
        previous = None
        row = []
        for b in range(blocks):
            after = picked[b + 1] if b + 1 < blocks else 0.0
            flow = adm4[b : b + 1] * (after - picked[b])
            received = 0.0 if previous is None else -previous
            flows = halves(jnp.where(low, *((received, flow) if b % 2 else (flow, received))), edges)
            previous = flow
            whole = dot(scaled[b], jac[b]) + dot_t(flows, hots[b])
            if b == 0:
                ends[0, here, :] = whole
            elif b == blocks - 1:
                ends[1, here, :] = whole
            else:
                rounded = whole.astype(BF16)
                mis[b, here, :] = rounded
                row.append((b, rounded))
        middle = pl.ds(1, blocks - 2)
        copy = pltpu.make_async_copy(mis.at[middle, here, :], mis_hbm.at[middle, here, :], sem)
        copy.start()
        sums = 0.0
        for k in range(0, len(row), 2):
            pair = row[k : k + 2]
            left = jnp.concatenate([value for _, value in pair], axis=1)
            first = pair[0][0]
            right = cond[first : first + len(pair)].reshape(len(pair) * width, cond.shape[2])
            sums = sums + dot(left, right)
        part[here, :] = sums
        copy.wait()

    row_chunks(total, 64, body)


def ends_kernel(dev, load, src, tgt, adm, cond, chip_in, pair_in, ends, part, keep, mis, out):
    blocks, total, width = dev.shape
    edges = src.shape[1]
    last = blocks - 1
    place, count = lax.axis_index("bus"), lax.axis_size("bus")
    even = place % 2 == 0
    ties = jnp.where(even, chip_in[total : total + TIE_ROWS, :].astype(F32), pair_in[total : total + TIE_ROWS, :].astype(F32))

    def twice(row):
        return jnp.concatenate([row[:, 0:edges]] * 2, axis=1)

    src_before = hot_columns(twice(ties[0:1]).astype(I32), width)
    tgt_before = hot_columns(twice(ties[1:2]).astype(I32), width)
    adm_before = twice(ties[2:3] + ties[3:4] + ties[4:5])
    adm_before = jnp.where(place == 0, 0.0, adm_before)
    src_last = hot_columns(twice(src[last : last + 1]), width)
    tgt_last = hot_columns(twice(tgt[last : last + 1]), width)
    adm_last = jnp.where(place == count - 1, 0.0, twice(adm[last : last + 1]))
    right = jnp.concatenate([cond[0], cond[last]], axis=0)
    reach = cond.shape[2]
    rate = keep[...]
    while rate.shape[0] > 1:
        half = rate.shape[0] // 2
        rate = rate[0:half] * rate[half : 2 * half]
    rate = folded(rate)
    upper = rate.astype(BF16).astype(F32)
    rate = jnp.concatenate([upper, rate - upper], axis=0)
    size = rate.shape[0]
    for k in range(0, total, 2 * size):
        out[k : k + 2 * size, reach : reach + 128] = jnp.concatenate([rate, rate], axis=0).astype(BF16)

    def body(here):
        pair_rows, chip_rows = pair_in[here, :].astype(F32), chip_in[here, :].astype(F32)
        following = jnp.where(even, pair_rows, chip_rows).astype(BF16)
        leading = jnp.where(even, chip_rows, pair_rows).astype(BF16)
        first = product(dev[0, here, :], load[0, here, :])
        flow_out = adm_last * dot(following, tgt_last)
        flow_in = adm_before * (dot(first, tgt_before) - dot(leading, src_before))
        low = (ends[0, here, :] - dot_t(halves(flow_in, edges), tgt_before)).astype(BF16)
        high = (ends[1, here, :] + dot_t(halves(flow_out, edges), src_last)).astype(BF16)
        mis[0, here, :] = low
        mis[1, here, :] = high
        sums = part[here, :] + dot(jnp.concatenate([low, high], axis=1), right)
        out[here, 0:reach] = sums.astype(BF16)

    row_chunks(total, 64, body)


def push_kernel(parts, gain, keep, states, running, rates, sent):
    count, rows, _ = parts.shape
    width = gain.shape[2]
    tiles = width // 128
    place, group = lax.axis_index("bus"), lax.axis_index("period")

    def add(k, total):
        return total + parts[k, :, 0:width].astype(F32)

    section_in = lax.fori_loop(0, count, add, jnp.zeros((rows, width), F32), unroll=8).astype(BF16)
    line = lax.broadcasted_iota(I32, (rows, width), 0)
    pushed = jnp.zeros((rows, width), F32)
    for r in range(rows):
        pushed = jnp.where(line == r, dot(section_in, gain[r]), pushed)
    rate, state = keep[...], pushed
    shift = 1
    while shift < rows:
        reached = line >= shift
        state = state + jnp.where(reached, rate * pltpu.roll(state, shift, 0), 0.0)
        rate = rate * jnp.where(reached, pltpu.roll(rate, shift, 0), 1.0)
        shift *= 2
    states[...] = state
    running[...] = rate

    def gather(k, carried):
        after, whole = carried
        both = parts[k, :, width : width + 128].astype(F32)
        span = both[0:tiles] + both[tiles : 2 * tiles]
        rates[k] = span
        return (after * jnp.where(k > place, span, 1.0), whole * span)

    ones = jnp.ones((tiles, 128), F32)
    after, whole = lax.fori_loop(0, count, gather, (ones, ones), unroll=8)
    upper = whole.astype(BF16).astype(F32)
    share = jnp.where(place % 2 == 0, upper, whole - upper)
    last_state = folded(state[rows - 1 : rows])
    here = jnp.concatenate([last_state, share], axis=0)
    beyond = jnp.concatenate([last_state * after, share], axis=0)
    for q in range(sent.shape[0] // count):
        value = jnp.where(group == q, here, beyond).astype(BF16)
        for k in range(count):
            sent[q * count + k] = value


def enter_kernel(spans, rates, states, running, outer, mis_in, out_hbm, mis, out, sems):
    blocks = mis.shape[0]
    copies = [pltpu.make_async_copy(outer.at[k], mis.at[k * (blocks - 1)], sems.at[k]) for k in range(2)]
    for copy in copies:
        copy.start()
    count, tiles, _ = rates.shape
    place, group = lax.axis_index("bus"), lax.axis_index("period")

    def add(k, total):
        return total + spans[k].astype(F32)

    entering = jnp.zeros((tiles, 128), F32)
    for q in range(spans.shape[0] // count - 1):
        first = q * count
        total = lax.fori_loop(first, first + count, add, jnp.zeros((2 * tiles, 128), F32), unroll=8)[0:tiles]
        pair = (spans[first].astype(F32) + spans[first + 1].astype(F32))[tiles : 2 * tiles]
        entering = jnp.where(q < group, pair * entering + total, entering)

    def step(k, entering):
        state = spans[group * count + k].astype(F32)[0:tiles]
        return jnp.where(k < place, rates[k] * entering + state, entering)

    entering = lax.fori_loop(0, count, step, entering, unroll=8)
    out[...] = states[...] + running[...] * unfolded(entering)
    copies.append(pltpu.make_async_copy(out, out_hbm, sems.at[2]))
    copies[2].start()
    for copy in copies:
        copy.wait()


def call(kernel, shapes, inputs, cost, scratch=(), specs=None, ins=None, aliases=None):
    single = not isinstance(shapes, (list, tuple))
    return pl.pallas_call(
        kernel,
        out_shape=shapes,
        in_specs=ins or [VM] * len(inputs),
        out_specs=specs or (VM if single else [VM] * len(shapes)),
        scratch_shapes=list(scratch),
        input_output_aliases=aliases or {},
        compiler_params=PARAMS,
        cost_estimate=pl.CostEstimate(flops=int(cost * 1e9), transcendentals=0, bytes_accessed=int(cost * 3.0e6)),
    )(*inputs)


def shards(deviation, loading, jacobian, tie_source, tie_target, tie_admittance, condense, section_gain, retention):
    blocks, total, width = deviation.shape
    states_width, edges = condense.shape[2], tie_source.shape[1]
    count = lax.axis_size("bus")
    spans = count * lax.axis_size("period")
    rows = section_gain.shape[1]
    shape = jax.ShapeDtypeStruct

    payload = shape((total + TIE_ROWS, width), BF16)
    pair_out, chip_out = call(
        halo_kernel,
        [payload, payload],
        [pltpu.with_memory_space_constraint(x, pltpu.HBM) for x in (deviation, loading, tie_source, tie_target, tie_admittance)],
        10.0,
        [
            pltpu.VMEM((2, total, width), BF16),
            pltpu.VMEM((2, total, width), BF16),
            pltpu.VMEM((blocks, edges), I32),
            pltpu.VMEM((blocks, edges), I32),
            pltpu.VMEM((blocks, edges), F32),
            pltpu.VMEM((TIE_ROWS, width), F32),
            pltpu.SemaphoreType.DMA((7,)),
        ],
        ins=[HBM] * 5,
    )
    pairs = [(k, k ^ 1) for k in range(count)]
    groups = lax.axis_size("period")
    chips = []
    for k in range(count):
        partner = k + 1 if k % 2 else k - 1
        for g in range(groups):
            if 0 <= partner < count:
                chips.append((k * groups + g, partner * groups + g))
            else:
                chips.append((k * groups + g, k * groups + g ^ 1))
    chip_in = lax.ppermute(chip_out, ("bus", "period"), chips)
    pair_in = lax.ppermute(pair_out, "bus", pairs)
    inner, ends, part = call(
        inner_kernel,
        [shape((blocks, total, width), BF16), shape((2, total, width), F32), shape((total, states_width), F32)],
        (deviation, loading, jacobian, tie_source, tie_target, tie_admittance, condense),
        5.0,
        [pltpu.VMEM((blocks, total, width), BF16), pltpu.SemaphoreType.DMA],
        [HBM, VM, VM],
    )
    outer, sums = call(
        ends_kernel,
        [shape((2, total, width), BF16), shape((total, states_width + 128), BF16)],
        (deviation, loading, tie_source, tie_target, tie_admittance, condense, chip_in, pair_in, ends, part, retention[0]),
        1.0,
    )
    parts = lax.all_to_all(sums.reshape(count, rows, states_width + 128), "bus", 0, 0, tiled=True)
    tiles = 2 * states_width // 128
    states, running, rates, sent = call(
        push_kernel,
        [
            shape((rows, states_width), F32),
            shape((rows, states_width), F32),
            shape((count, tiles // 2, 128), F32),
            shape((spans, tiles, 128), BF16),
        ],
        (parts, section_gain[0], retention[0]),
        2.0,
    )
    everything = lax.all_to_all(sent, ("period", "bus"), 0, 0, tiled=True)
    out, mismatch = call(
        enter_kernel,
        [shape((rows, states_width), F32), shape((blocks, total, width), BF16)],
        (everything, rates, states, running, outer, inner),
        1.0,
        [pltpu.VMEM((rows, states_width), F32), pltpu.SemaphoreType.DMA((3,))],
        [HBM, HBM],
        [VM] * 5 + [HBM],
        {5: 1},
    )
    return (mismatch, out[None])


def solution(mesh):
    placed = (
        P("bus", "period", None),
        P("bus", "period", None),
        P("bus", None, None),
        P("bus", None),
        P("bus", None),
        P("bus", None),
        P("bus", None, None),
        P("period", "bus", None, None),
        P("period", "bus", None),
    )
    return jax.shard_map(
        shards,
        mesh=mesh,
        in_specs=placed,
        out_specs=(P("bus", "period", None), P("period", "bus", None)),
        check_vma=False,
    )
```

```python
import jax
import jax.numpy as jnp
from jax import lax
from jax.experimental import pallas as pl
from jax.experimental.pallas import tpu as pltpu
from jax.sharding import PartitionSpec as P

F32, BF16, I32 = jnp.float32, jnp.bfloat16, jnp.int32
VM = pl.BlockSpec(memory_space=pltpu.VMEM)
TIE_ROWS = 16
SUMMED_ROWS = 2
PARAMS = pltpu.CompilerParams(vmem_limit_bytes=16 * 1024 * 1024)
HBM = pl.BlockSpec(memory_space=pltpu.HBM)


def dot(a, b):
    return jnp.dot(a, b, preferred_element_type=F32)


def dot_t(a, b):
    return lax.dot_general(a, b, (((1,), (1,)), ((), ())), preferred_element_type=F32)


def product(deviation, loading):
    return (deviation.astype(F32) * loading.astype(F32)).astype(BF16)


def hot_columns(index_row, width):
    rows = lax.broadcasted_iota(I32, (width, index_row.shape[1]), 0)
    return (rows == index_row).astype(F32).astype(BF16)


def halves(flow, edges):
    upper = flow.astype(BF16).astype(F32)
    lane = lax.broadcasted_iota(I32, flow.shape, 1)
    return jnp.where(lane % (2 * edges) < edges, upper, flow - upper).astype(BF16)


def folded(row):
    return jnp.concatenate([row[:, 128 * k : 128 * k + 128] for k in range(row.shape[1] // 128)], axis=0)


def unfolded(rows):
    return jnp.concatenate([rows[k : k + 1] for k in range(rows.shape[0])], axis=1)


def row_chunks(total, size, body):
    if total <= size:
        body(pl.ds(0, total))
        return

    @pl.loop(0, total // size)
    def _(k):
        body(pl.ds(pl.multiple_of(k * size, size), size))


def halo_kernel(dev_hbm, load_hbm, src_hbm, tgt_hbm, adm_hbm, pair_out, chip_out, src, tgt, adm, dev, load, ties, sems):
    last = dev_hbm.shape[0] - 1
    rows = dev.shape[1]
    edges = src.shape[1]
    fetches = [
        pltpu.make_async_copy(source, target, sems.at[k])
        for k, (source, target) in enumerate(
            [
                (dev_hbm.at[0], dev.at[0]),
                (dev_hbm.at[last], dev.at[1]),
                (load_hbm.at[0], load.at[0]),
                (load_hbm.at[last], load.at[1]),
                (src_hbm, src),
                (tgt_hbm, tgt),
                (adm_hbm, adm),
            ]
        )
    ]
    for fetch in fetches:
        fetch.start()
    even = lax.axis_index("bus") % 2 == 0
    ties[...] = jnp.zeros_like(ties)
    for fetch in fetches:
        fetch.wait()
    a = adm[last : last + 1, :]
    high = a.astype(BF16).astype(F32)
    mid = (a - high).astype(BF16).astype(F32)
    ties[0:1, 0:edges] = src[last : last + 1, :].astype(F32)
    ties[1:2, 0:edges] = tgt[last : last + 1, :].astype(F32)
    ties[2:3, 0:edges] = high
    ties[3:4, 0:edges] = mid
    ties[4:5, 0:edges] = a - high - mid
    packed = ties[...].astype(BF16)

    first, final = product(dev[0], load[0]).astype(F32), product(dev[1], load[1]).astype(F32)
    pair_out[0:rows, :] = jnp.where(even, final, first).astype(BF16)
    chip_out[0:rows, :] = jnp.where(even, first, final).astype(BF16)
    pair_out[rows : rows + TIE_ROWS, :] = packed
    chip_out[rows : rows + TIE_ROWS, :] = packed


def pass_kernel(given, same):
    same[0:8, :] = given[0:8, :]


def inner_kernel(dev, load, jac, src, tgt, adm, cond, mis_hbm, ends, part, mis, sem):
    blocks, total, width = dev.shape
    edges = src.shape[1]
    src4 = jnp.concatenate([src[...]] * 4, axis=1)
    tgt4 = jnp.concatenate([tgt[...]] * 4, axis=1)
    adm4 = jnp.concatenate([adm[...]] * 4, axis=1)
    low = lax.broadcasted_iota(I32, (1, 4 * edges), 1) < 2 * edges
    hots = []
    for b in range(blocks):
        before = tgt4[b - 1 : b] if b else jnp.full((1, 4 * edges), -1, I32)
        mine = src4[b : b + 1]
        hots.append(hot_columns(jnp.where(low, *((before, mine) if b % 2 else (mine, before))), width))

    def body(here):
        scaled = [product(dev[b, here, :], load[b, here, :]) for b in range(blocks)]
        picked = [dot(scaled[b], hots[b]) for b in range(blocks)]
        previous = None
        row = []
        for b in range(blocks):
            after = picked[b + 1] if b + 1 < blocks else 0.0
            flow = adm4[b : b + 1] * (after - picked[b])
            received = 0.0 if previous is None else -previous
            flows = halves(jnp.where(low, *((received, flow) if b % 2 else (flow, received))), edges)
            previous = flow
            whole = dot(scaled[b], jac[b]) + dot_t(flows, hots[b])
            if b == 0:
                ends[0, here, :] = whole
            elif b == blocks - 1:
                ends[1, here, :] = whole
            else:
                rounded = whole.astype(BF16)
                mis[b, here, :] = rounded
                row.append((b, rounded))
        middle = pl.ds(1, blocks - 2)
        copy = pltpu.make_async_copy(mis.at[middle, here, :], mis_hbm.at[middle, here, :], sem)
        copy.start()
        sums = 0.0
        for k in range(0, len(row), 2):
            pair = row[k : k + 2]
            left = jnp.concatenate([value for _, value in pair], axis=1)
            first = pair[0][0]
            right = cond[first : first + len(pair)].reshape(len(pair) * width, cond.shape[2])
            sums = sums + dot(left, right)
        part[here, :] = sums
        copy.wait()

    row_chunks(total, 64, body)


def ends_kernel(dev, load, src, tgt, adm, cond, chip_in, pair_in, ends, part, keep, mis, out):
    blocks, total, width = dev.shape
    edges = src.shape[1]
    last = blocks - 1
    place, count = lax.axis_index("bus"), lax.axis_size("bus")
    even = place % 2 == 0
    ties = jnp.where(even, chip_in[total : total + TIE_ROWS, :].astype(F32), pair_in[total : total + TIE_ROWS, :].astype(F32))

    def twice(row):
        return jnp.concatenate([row[:, 0:edges]] * 2, axis=1)

    src_before = hot_columns(twice(ties[0:1]).astype(I32), width)
    tgt_before = hot_columns(twice(ties[1:2]).astype(I32), width)
    adm_before = twice(ties[2:3] + ties[3:4] + ties[4:5])
    adm_before = jnp.where(place == 0, 0.0, adm_before)
    src_last = hot_columns(twice(src[last : last + 1]), width)
    tgt_last = hot_columns(twice(tgt[last : last + 1]), width)
    adm_last = jnp.where(place == count - 1, 0.0, twice(adm[last : last + 1]))
    right = jnp.concatenate([cond[0], cond[last]], axis=0)
    reach = cond.shape[2]
    rate = keep[...]
    while rate.shape[0] > 1:
        half = rate.shape[0] // 2
        rate = rate[0:half] * rate[half : 2 * half]
    rate = folded(rate)
    upper = rate.astype(BF16).astype(F32)
    rate = jnp.concatenate([upper, rate - upper], axis=0)
    size = rate.shape[0]
    for k in range(0, total, 2 * size):
        out[k : k + 2 * size, reach : reach + 128] = jnp.concatenate([rate, rate], axis=0).astype(BF16)

    def body(here):
        pair_rows, chip_rows = pair_in[here, :].astype(F32), chip_in[here, :].astype(F32)
        following = jnp.where(even, pair_rows, chip_rows).astype(BF16)
        leading = jnp.where(even, chip_rows, pair_rows).astype(BF16)
        first = product(dev[0, here, :], load[0, here, :])
        flow_out = adm_last * dot(following, tgt_last)
        flow_in = adm_before * (dot(first, tgt_before) - dot(leading, src_before))
        low = (ends[0, here, :] - dot_t(halves(flow_in, edges), tgt_before)).astype(BF16)
        high = (ends[1, here, :] + dot_t(halves(flow_out, edges), src_last)).astype(BF16)
        mis[0, here, :] = low
        mis[1, here, :] = high
        sums = part[here, :] + dot(jnp.concatenate([low, high], axis=1), right)
        out[here, 0:reach] = sums.astype(BF16)

    row_chunks(total, 64, body)


def push_kernel(parts, gain, keep, states, running, rates, sent):
    count, rows, _ = parts.shape
    width = gain.shape[2]
    tiles = width // 128
    place, group = lax.axis_index("bus"), lax.axis_index("period")

    def add(k, total):
        return total + parts[k, :, 0:width].astype(F32)

    section_in = lax.fori_loop(0, count, add, jnp.zeros((rows, width), F32), unroll=8).astype(BF16)
    line = lax.broadcasted_iota(I32, (rows, width), 0)
    columns = jnp.transpose(section_in.astype(F32))
    pushed = jnp.zeros((rows, width), F32)
    for r in range(rows):
        if r < rows - SUMMED_ROWS:
            row = dot(section_in, gain[r])
        else:
            row = jnp.zeros((16, width), F32)
            for m in range(0, width, 16):
                row = row + gain[r, m : m + 16, :].astype(F32) * columns[m : m + 16, r : r + 1]
            row = jnp.sum(row, axis=0, keepdims=True)
        pushed = jnp.where(line == r, row, pushed)
    rate, state = keep[...], pushed
    shift = 1
    while shift < rows:
        reached = line >= shift
        state = state + jnp.where(reached, rate * pltpu.roll(state, shift, 0), 0.0)
        rate = rate * jnp.where(reached, pltpu.roll(rate, shift, 0), 1.0)
        shift *= 2
    states[...] = state
    running[...] = rate

    def gather(k, carried):
        after, whole = carried
        both = parts[k, :, width : width + 128].astype(F32)
        span = both[0:tiles] + both[tiles : 2 * tiles]
        rates[k] = span
        return (after * jnp.where(k > place, span, 1.0), whole * span)

    ones = jnp.ones((tiles, 128), F32)
    after, whole = lax.fori_loop(0, count, gather, (ones, ones), unroll=8)
    upper = whole.astype(BF16).astype(F32)
    share = jnp.where(place % 2 == 0, upper, whole - upper)
    last_state = folded(state[rows - 1 : rows])
    here = jnp.concatenate([last_state, share], axis=0)
    beyond = jnp.concatenate([last_state * after, share], axis=0)
    for q in range(sent.shape[0] // count):
        value = jnp.where(group == q, here, beyond).astype(BF16)
        for k in range(count):
            sent[q * count + k] = value


def enter_kernel(spans, rates, states, running, outer, mis_in, out_hbm, mis, out, sems):
    blocks = mis.shape[0]
    copies = [pltpu.make_async_copy(outer.at[k], mis.at[k * (blocks - 1)], sems.at[k]) for k in range(2)]
    for copy in copies:
        copy.start()
    count, tiles, _ = rates.shape
    place, group = lax.axis_index("bus"), lax.axis_index("period")

    def add(k, total):
        return total + spans[k].astype(F32)

    entering = jnp.zeros((tiles, 128), F32)
    for q in range(spans.shape[0] // count - 1):
        first = q * count
        total = lax.fori_loop(first, first + count, add, jnp.zeros((2 * tiles, 128), F32), unroll=8)[0:tiles]
        pair = (spans[first].astype(F32) + spans[first + 1].astype(F32))[tiles : 2 * tiles]
        entering = jnp.where(q < group, pair * entering + total, entering)

    def step(k, entering):
        state = spans[group * count + k].astype(F32)[0:tiles]
        return jnp.where(k < place, rates[k] * entering + state, entering)

    entering = lax.fori_loop(0, count, step, entering, unroll=8)
    out[...] = states[...] + running[...] * unfolded(entering)
    copies.append(pltpu.make_async_copy(out, out_hbm, sems.at[2]))
    copies[2].start()
    for copy in copies:
        copy.wait()


def call(kernel, shapes, inputs, cost, scratch=(), specs=None, ins=None, aliases=None):
    single = not isinstance(shapes, (list, tuple))
    return pl.pallas_call(
        kernel,
        out_shape=shapes,
        in_specs=ins or [VM] * len(inputs),
        out_specs=specs or (VM if single else [VM] * len(shapes)),
        scratch_shapes=list(scratch),
        input_output_aliases=aliases or {},
        compiler_params=PARAMS,
        cost_estimate=pl.CostEstimate(flops=int(cost * 1e9), transcendentals=0, bytes_accessed=int(cost * 3.0e6)),
    )(*inputs)


def shards(deviation, loading, jacobian, tie_source, tie_target, tie_admittance, condense, section_gain, retention):
    blocks, total, width = deviation.shape
    states_width, edges = condense.shape[2], tie_source.shape[1]
    count = lax.axis_size("bus")
    spans = count * lax.axis_size("period")
    rows = section_gain.shape[1]
    shape = jax.ShapeDtypeStruct

    payload = shape((total + TIE_ROWS, width), BF16)
    lines, weights = shape((blocks, edges), I32), shape((blocks, edges), F32)
    pair_out, chip_out, src, tgt, adm = call(
        halo_kernel,
        [payload, payload, lines, lines, weights],
        [pltpu.with_memory_space_constraint(x, pltpu.HBM) for x in (deviation, loading, tie_source, tie_target, tie_admittance)],
        0.1,
        [
            pltpu.VMEM((2, total, width), BF16),
            pltpu.VMEM((2, total, width), BF16),
            pltpu.VMEM((TIE_ROWS, width), F32),
            pltpu.SemaphoreType.DMA((7,)),
        ],
        ins=[HBM] * 5,
    )
    chip_out = call(pass_kernel, payload, (chip_out,), 10.0, aliases={0: 0})
    pairs = [(k, k ^ 1) for k in range(count)]
    groups = lax.axis_size("period")
    chips = []
    for k in range(count):
        partner = k + 1 if k % 2 else k - 1
        for g in range(groups):
            if 0 <= partner < count:
                chips.append((k * groups + g, partner * groups + g))
            else:
                chips.append((k * groups + g, k * groups + g ^ 1))
    chip_in = lax.ppermute(chip_out, ("bus", "period"), chips)
    pair_in = lax.ppermute(pair_out, "bus", pairs)
    inner, ends, part = call(
        inner_kernel,
        [shape((blocks, total, width), BF16), shape((2, total, width), F32), shape((total, states_width), F32)],
        (deviation, loading, jacobian, src, tgt, adm, condense),
        5.0,
        [pltpu.VMEM((blocks, total, width), BF16), pltpu.SemaphoreType.DMA],
        [HBM, VM, VM],
    )
    outer, sums = call(
        ends_kernel,
        [shape((2, total, width), BF16), shape((total, states_width + 128), BF16)],
        (deviation, loading, src, tgt, adm, condense, chip_in, pair_in, ends, part, retention[0]),
        1.0,
    )
    parts = lax.all_to_all(sums.reshape(count, rows, states_width + 128), "bus", 0, 0, tiled=True)
    tiles = 2 * states_width // 128
    states, running, rates, sent = call(
        push_kernel,
        [
            shape((rows, states_width), F32),
            shape((rows, states_width), F32),
            shape((count, tiles // 2, 128), F32),
            shape((spans, tiles, 128), BF16),
        ],
        (parts, section_gain[0], retention[0]),
        2.0,
    )
    everything = lax.all_to_all(sent, ("period", "bus"), 0, 0, tiled=True)
    out, mismatch = call(
        enter_kernel,
        [shape((rows, states_width), F32), shape((blocks, total, width), BF16)],
        (everything, rates, states, running, outer, inner),
        1.0,
        [pltpu.VMEM((rows, states_width), F32), pltpu.SemaphoreType.DMA((3,))],
        [HBM, HBM],
        [VM] * 5 + [HBM],
        {5: 1},
    )
    return (mismatch, out[None])


def solution(mesh):
    placed = (
        P("bus", "period", None),
        P("bus", "period", None),
        P("bus", None, None),
        P("bus", None),
        P("bus", None),
        P("bus", None),
        P("bus", None, None),
        P("period", "bus", None, None),
        P("period", "bus", None),
    )
    return jax.shard_map(
        shards,
        mesh=mesh,
        in_specs=placed,
        out_specs=(P("bus", "period", None), P("period", "bus", None)),
        check_vma=False,
    )
```

```python
import jax
import jax.numpy as jnp
from jax import lax
from jax.experimental import pallas as pl
from jax.experimental.pallas import tpu as pltpu
from jax.sharding import PartitionSpec as P

F32, BF16, I32 = jnp.float32, jnp.bfloat16, jnp.int32
VM = pl.BlockSpec(memory_space=pltpu.VMEM)
TIE_ROWS = 16
SUMMED_ROWS = 2
PARAMS = pltpu.CompilerParams(vmem_limit_bytes=16 * 1024 * 1024)
HBM = pl.BlockSpec(memory_space=pltpu.HBM)


def dot(a, b):
    return jnp.dot(a, b, preferred_element_type=F32)


def dot_t(a, b):
    return lax.dot_general(a, b, (((1,), (1,)), ((), ())), preferred_element_type=F32)


def product(deviation, loading):
    return (deviation.astype(F32) * loading.astype(F32)).astype(BF16)


def hot_columns(index_row, width):
    rows = lax.broadcasted_iota(I32, (width, index_row.shape[1]), 0)
    return (rows == index_row).astype(F32).astype(BF16)


def halves(flow, edges):
    upper = flow.astype(BF16).astype(F32)
    lane = lax.broadcasted_iota(I32, flow.shape, 1)
    return jnp.where(lane % (2 * edges) < edges, upper, flow - upper).astype(BF16)


def folded(row):
    return jnp.concatenate([row[:, 128 * k : 128 * k + 128] for k in range(row.shape[1] // 128)], axis=0)


def unfolded(rows):
    return jnp.concatenate([rows[k : k + 1] for k in range(rows.shape[0])], axis=1)


def row_chunks(total, size, body):
    if total <= size:
        body(pl.ds(0, total))
        return

    @pl.loop(0, total // size)
    def _(k):
        body(pl.ds(pl.multiple_of(k * size, size), size))


def halo_kernel(dev_hbm, load_hbm, src_hbm, tgt_hbm, adm_hbm, pair_out, chip_out, dev, load, src, tgt, adm, ties, sems):
    last = dev_hbm.shape[0] - 1
    rows = dev.shape[1]
    edges = src.shape[1]
    fetches = [
        pltpu.make_async_copy(source, target, sems.at[k])
        for k, (source, target) in enumerate(
            [
                (dev_hbm.at[0], dev.at[0]),
                (dev_hbm.at[last], dev.at[1]),
                (load_hbm.at[0], load.at[0]),
                (load_hbm.at[last], load.at[1]),
                (src_hbm, src),
                (tgt_hbm, tgt),
                (adm_hbm, adm),
            ]
        )
    ]
    for fetch in fetches:
        fetch.start()
    even = lax.axis_index("bus") % 2 == 0
    ties[...] = jnp.zeros_like(ties)
    for fetch in fetches:
        fetch.wait()
    a = adm[last : last + 1, :]
    high = a.astype(BF16).astype(F32)
    mid = (a - high).astype(BF16).astype(F32)
    ties[0:1, 0:edges] = src[last : last + 1, :].astype(F32)
    ties[1:2, 0:edges] = tgt[last : last + 1, :].astype(F32)
    ties[2:3, 0:edges] = high
    ties[3:4, 0:edges] = mid
    ties[4:5, 0:edges] = a - high - mid
    packed = ties[...].astype(BF16)

    first, final = product(dev[0], load[0]).astype(F32), product(dev[1], load[1]).astype(F32)
    pair_out[0:rows, :] = jnp.where(even, final, first).astype(BF16)
    chip_out[0:rows, :] = jnp.where(even, first, final).astype(BF16)
    pair_out[rows : rows + TIE_ROWS, :] = packed
    chip_out[rows : rows + TIE_ROWS, :] = packed


def inner_kernel(dev, load, jac, src, tgt, adm, cond, mis_hbm, ends, part, mis, sem):
    blocks, total, width = dev.shape
    edges = src.shape[1]
    src4 = jnp.concatenate([src[...]] * 4, axis=1)
    tgt4 = jnp.concatenate([tgt[...]] * 4, axis=1)
    adm4 = jnp.concatenate([adm[...]] * 4, axis=1)
    low = lax.broadcasted_iota(I32, (1, 4 * edges), 1) < 2 * edges
    hots = []
    for b in range(blocks):
        before = tgt4[b - 1 : b] if b else jnp.full((1, 4 * edges), -1, I32)
        mine = src4[b : b + 1]
        hots.append(hot_columns(jnp.where(low, *((before, mine) if b % 2 else (mine, before))), width))

    def body(here):
        scaled = [product(dev[b, here, :], load[b, here, :]) for b in range(blocks)]
        picked = [dot(scaled[b], hots[b]) for b in range(blocks)]
        previous = None
        row = []
        for b in range(blocks):
            after = picked[b + 1] if b + 1 < blocks else 0.0
            flow = adm4[b : b + 1] * (after - picked[b])
            received = 0.0 if previous is None else -previous
            flows = halves(jnp.where(low, *((received, flow) if b % 2 else (flow, received))), edges)
            previous = flow
            whole = dot(scaled[b], jac[b]) + dot_t(flows, hots[b])
            if b == 0:
                ends[0, here, :] = whole
            elif b == blocks - 1:
                ends[1, here, :] = whole
            else:
                rounded = whole.astype(BF16)
                mis[b, here, :] = rounded
                row.append((b, rounded))
        middle = pl.ds(1, blocks - 2)
        copy = pltpu.make_async_copy(mis.at[middle, here, :], mis_hbm.at[middle, here, :], sem)
        copy.start()
        sums = 0.0
        for k in range(0, len(row), 2):
            pair = row[k : k + 2]
            left = jnp.concatenate([value for _, value in pair], axis=1)
            first = pair[0][0]
            right = cond[first : first + len(pair)].reshape(len(pair) * width, cond.shape[2])
            sums = sums + dot(left, right)
        part[here, :] = sums
        copy.wait()

    row_chunks(total, 64, body)


def ends_kernel(dev, load, src, tgt, adm, cond, chip_in, pair_in, ends, part, keep, mis, out):
    blocks, total, width = dev.shape
    edges = src.shape[1]
    last = blocks - 1
    place, count = lax.axis_index("bus"), lax.axis_size("bus")
    even = place % 2 == 0
    ties = jnp.where(even, chip_in[total : total + TIE_ROWS, :].astype(F32), pair_in[total : total + TIE_ROWS, :].astype(F32))

    def twice(row):
        return jnp.concatenate([row[:, 0:edges]] * 2, axis=1)

    src_before = hot_columns(twice(ties[0:1]).astype(I32), width)
    tgt_before = hot_columns(twice(ties[1:2]).astype(I32), width)
    adm_before = twice(ties[2:3] + ties[3:4] + ties[4:5])
    adm_before = jnp.where(place == 0, 0.0, adm_before)
    src_last = hot_columns(twice(src[last : last + 1]), width)
    tgt_last = hot_columns(twice(tgt[last : last + 1]), width)
    adm_last = jnp.where(place == count - 1, 0.0, twice(adm[last : last + 1]))
    right = jnp.concatenate([cond[0], cond[last]], axis=0)
    reach = cond.shape[2]
    rate = keep[...]
    while rate.shape[0] > 1:
        half = rate.shape[0] // 2
        rate = rate[0:half] * rate[half : 2 * half]
    rate = folded(rate)
    upper = rate.astype(BF16).astype(F32)
    rate = jnp.concatenate([upper, rate - upper], axis=0)
    size = rate.shape[0]
    for k in range(0, total, 2 * size):
        out[k : k + 2 * size, reach : reach + 128] = jnp.concatenate([rate, rate], axis=0).astype(BF16)

    def body(here):
        pair_rows, chip_rows = pair_in[here, :].astype(F32), chip_in[here, :].astype(F32)
        following = jnp.where(even, pair_rows, chip_rows).astype(BF16)
        leading = jnp.where(even, chip_rows, pair_rows).astype(BF16)
        first = product(dev[0, here, :], load[0, here, :])
        flow_out = adm_last * dot(following, tgt_last)
        flow_in = adm_before * (dot(first, tgt_before) - dot(leading, src_before))
        low = (ends[0, here, :] - dot_t(halves(flow_in, edges), tgt_before)).astype(BF16)
        high = (ends[1, here, :] + dot_t(halves(flow_out, edges), src_last)).astype(BF16)
        mis[0, here, :] = low
        mis[1, here, :] = high
        sums = part[here, :] + dot(jnp.concatenate([low, high], axis=1), right)
        out[here, 0:reach] = sums.astype(BF16)

    row_chunks(total, 64, body)


def push_kernel(parts, gain, keep, states, running, rates, sent):
    count, rows, _ = parts.shape
    width = gain.shape[2]
    tiles = width // 128
    place, group = lax.axis_index("bus"), lax.axis_index("period")

    def add(k, total):
        return total + parts[k, :, 0:width].astype(F32)

    section_in = lax.fori_loop(0, count, add, jnp.zeros((rows, width), F32), unroll=8).astype(BF16)
    line = lax.broadcasted_iota(I32, (rows, width), 0)
    columns = jnp.transpose(section_in.astype(F32))
    pushed = jnp.zeros((rows, width), F32)
    for r in range(rows):
        if r < rows - SUMMED_ROWS:
            row = dot(section_in, gain[r])
        else:
            row = jnp.zeros((16, width), F32)
            for m in range(0, width, 16):
                row = row + gain[r, m : m + 16, :].astype(F32) * columns[m : m + 16, r : r + 1]
            row = jnp.sum(row, axis=0, keepdims=True)
        pushed = jnp.where(line == r, row, pushed)
    rate, state = keep[...], pushed
    shift = 1
    while shift < rows:
        reached = line >= shift
        state = state + jnp.where(reached, rate * pltpu.roll(state, shift, 0), 0.0)
        rate = rate * jnp.where(reached, pltpu.roll(rate, shift, 0), 1.0)
        shift *= 2
    states[...] = state
    running[...] = rate

    def gather(k, carried):
        after, whole = carried
        both = parts[k, :, width : width + 128].astype(F32)
        span = both[0:tiles] + both[tiles : 2 * tiles]
        rates[k] = span
        return (after * jnp.where(k > place, span, 1.0), whole * span)

    ones = jnp.ones((tiles, 128), F32)
    after, whole = lax.fori_loop(0, count, gather, (ones, ones), unroll=8)
    upper = whole.astype(BF16).astype(F32)
    share = jnp.where(place % 2 == 0, upper, whole - upper)
    last_state = folded(state[rows - 1 : rows])
    here = jnp.concatenate([last_state, share], axis=0)
    beyond = jnp.concatenate([last_state * after, share], axis=0)
    for q in range(sent.shape[0] // count):
        value = jnp.where(group == q, here, beyond).astype(BF16)
        for k in range(count):
            sent[q * count + k] = value


def enter_kernel(spans, rates, states, running, outer, mis_in, out_hbm, mis, out, sems):
    blocks = mis.shape[0]
    copies = [pltpu.make_async_copy(outer.at[k], mis.at[k * (blocks - 1)], sems.at[k]) for k in range(2)]
    for copy in copies:
        copy.start()
    count, tiles, _ = rates.shape
    place, group = lax.axis_index("bus"), lax.axis_index("period")

    def add(k, total):
        return total + spans[k].astype(F32)

    entering = jnp.zeros((tiles, 128), F32)
    for q in range(spans.shape[0] // count - 1):
        first = q * count
        total = lax.fori_loop(first, first + count, add, jnp.zeros((2 * tiles, 128), F32), unroll=8)[0:tiles]
        pair = (spans[first].astype(F32) + spans[first + 1].astype(F32))[tiles : 2 * tiles]
        entering = jnp.where(q < group, pair * entering + total, entering)

    def step(k, entering):
        state = spans[group * count + k].astype(F32)[0:tiles]
        return jnp.where(k < place, rates[k] * entering + state, entering)

    entering = lax.fori_loop(0, count, step, entering, unroll=8)
    out[...] = states[...] + running[...] * unfolded(entering)
    copies.append(pltpu.make_async_copy(out, out_hbm, sems.at[2]))
    copies[2].start()
    for copy in copies:
        copy.wait()


def call(kernel, shapes, inputs, cost, scratch=(), specs=None, ins=None, aliases=None):
    single = not isinstance(shapes, (list, tuple))
    return pl.pallas_call(
        kernel,
        out_shape=shapes,
        in_specs=ins or [VM] * len(inputs),
        out_specs=specs or (VM if single else [VM] * len(shapes)),
        scratch_shapes=list(scratch),
        input_output_aliases=aliases or {},
        compiler_params=PARAMS,
        cost_estimate=pl.CostEstimate(flops=int(cost * 1e9), transcendentals=0, bytes_accessed=int(cost * 3.0e6)),
    )(*inputs)


def shards(deviation, loading, jacobian, tie_source, tie_target, tie_admittance, condense, section_gain, retention):
    blocks, total, width = deviation.shape
    states_width, edges = condense.shape[2], tie_source.shape[1]
    count = lax.axis_size("bus")
    spans = count * lax.axis_size("period")
    rows = section_gain.shape[1]
    shape = jax.ShapeDtypeStruct

    payload = shape((total + TIE_ROWS, width), BF16)
    pair_out, chip_out = call(
        halo_kernel,
        [payload, payload],
        [pltpu.with_memory_space_constraint(x, pltpu.HBM) for x in (deviation, loading, tie_source, tie_target, tie_admittance)],
        10.0,
        [
            pltpu.VMEM((2, total, width), BF16),
            pltpu.VMEM((2, total, width), BF16),
            pltpu.VMEM((blocks, edges), I32),
            pltpu.VMEM((blocks, edges), I32),
            pltpu.VMEM((blocks, edges), F32),
            pltpu.VMEM((TIE_ROWS, width), F32),
            pltpu.SemaphoreType.DMA((7,)),
        ],
        ins=[HBM] * 5,
    )
    pairs = [(k, k ^ 1) for k in range(count)]
    groups = lax.axis_size("period")
    chips = []
    for k in range(count):
        partner = k + 1 if k % 2 else k - 1
        for g in range(groups):
            if 0 <= partner < count:
                chips.append((k * groups + g, partner * groups + g))
            else:
                chips.append((k * groups + g, k * groups + g ^ 1))
    chip_in = lax.ppermute(chip_out, ("bus", "period"), chips)
    pair_in = lax.ppermute(pair_out, "bus", pairs)
    inner, ends, part = call(
        inner_kernel,
        [shape((blocks, total, width), BF16), shape((2, total, width), F32), shape((total, states_width), F32)],
        (deviation, loading, jacobian, tie_source, tie_target, tie_admittance, condense),
        5.0,
        [pltpu.VMEM((blocks, total, width), BF16), pltpu.SemaphoreType.DMA],
        [HBM, VM, VM],
    )
    outer, sums = call(
        ends_kernel,
        [shape((2, total, width), BF16), shape((total, states_width + 128), BF16)],
        (deviation, loading, tie_source, tie_target, tie_admittance, condense, chip_in, pair_in, ends, part, retention[0]),
        1.0,
    )
    parts = lax.all_to_all(sums.reshape(count, rows, states_width + 128), "bus", 0, 0, tiled=True)
    tiles = 2 * states_width // 128
    states, running, rates, sent = call(
        push_kernel,
        [
            shape((rows, states_width), F32),
            shape((rows, states_width), F32),
            shape((count, tiles // 2, 128), F32),
            shape((spans, tiles, 128), BF16),
        ],
        (parts, section_gain[0], retention[0]),
        2.0,
    )
    everything = lax.all_to_all(sent, ("period", "bus"), 0, 0, tiled=True)
    out, mismatch = call(
        enter_kernel,
        [shape((rows, states_width), F32), shape((blocks, total, width), BF16)],
        (everything, rates, states, running, outer, inner),
        1.0,
        [pltpu.VMEM((rows, states_width), F32), pltpu.SemaphoreType.DMA((3,))],
        [HBM, HBM],
        [VM] * 5 + [HBM],
        {5: 1},
    )
    return (mismatch, out[None])


def solution(mesh):
    placed = (
        P("bus", "period", None),
        P("bus", "period", None),
        P("bus", None, None),
        P("bus", None),
        P("bus", None),
        P("bus", None),
        P("bus", None, None),
        P("period", "bus", None, None),
        P("period", "bus", None),
    )
    return jax.shard_map(
        shards,
        mesh=mesh,
        in_specs=placed,
        out_specs=(P("bus", "period", None), P("period", "bus", None)),
        check_vma=False,
    )
```

```python
import jax
import jax.numpy as jnp
from jax import lax
from jax.experimental import pallas as pl
from jax.experimental.pallas import tpu as pltpu
from jax.sharding import PartitionSpec as P

F32, BF16, I32 = jnp.float32, jnp.bfloat16, jnp.int32
VM = pl.BlockSpec(memory_space=pltpu.VMEM)
TIE_ROWS = 16
SUMMED_ROWS = 2
PARAMS = pltpu.CompilerParams(vmem_limit_bytes=16 * 1024 * 1024)
HBM = pl.BlockSpec(memory_space=pltpu.HBM)


def dot(a, b):
    return jnp.dot(a, b, preferred_element_type=F32)


def dot_t(a, b):
    return lax.dot_general(a, b, (((1,), (1,)), ((), ())), preferred_element_type=F32)


def product(deviation, loading):
    return (deviation.astype(F32) * loading.astype(F32)).astype(BF16)


def hot_columns(index_row, width):
    rows = lax.broadcasted_iota(I32, (width, index_row.shape[1]), 0)
    return (rows == index_row).astype(F32).astype(BF16)


def halves(flow, edges):
    upper = flow.astype(BF16).astype(F32)
    lane = lax.broadcasted_iota(I32, flow.shape, 1)
    return jnp.where(lane % (2 * edges) < edges, upper, flow - upper).astype(BF16)


def folded(row):
    return jnp.concatenate([row[:, 128 * k : 128 * k + 128] for k in range(row.shape[1] // 128)], axis=0)


def unfolded(rows):
    return jnp.concatenate([rows[k : k + 1] for k in range(rows.shape[0])], axis=1)


def row_chunks(total, size, body):
    if total <= size:
        body(pl.ds(0, total))
        return

    @pl.loop(0, total // size)
    def _(k):
        body(pl.ds(pl.multiple_of(k * size, size), size))


def halo_kernel(dev_hbm, load_hbm, src_hbm, tgt_hbm, adm_hbm, pair_out, chip_out, src, tgt, adm, dev, load, ties, sems):
    last = dev_hbm.shape[0] - 1
    rows = dev.shape[1]
    edges = src.shape[1]
    fetches = [
        pltpu.make_async_copy(source, target, sems.at[k])
        for k, (source, target) in enumerate(
            [
                (dev_hbm.at[0], dev.at[0]),
                (dev_hbm.at[last], dev.at[1]),
                (load_hbm.at[0], load.at[0]),
                (load_hbm.at[last], load.at[1]),
                (src_hbm, src),
                (tgt_hbm, tgt),
                (adm_hbm, adm),
            ]
        )
    ]
    for fetch in fetches:
        fetch.start()
    even = lax.axis_index("bus") % 2 == 0
    ties[...] = jnp.zeros_like(ties)
    for fetch in fetches:
        fetch.wait()
    a = adm[last : last + 1, :]
    high = a.astype(BF16).astype(F32)
    mid = (a - high).astype(BF16).astype(F32)
    ties[0:1, 0:edges] = src[last : last + 1, :].astype(F32)
    ties[1:2, 0:edges] = tgt[last : last + 1, :].astype(F32)
    ties[2:3, 0:edges] = high
    ties[3:4, 0:edges] = mid
    ties[4:5, 0:edges] = a - high - mid
    packed = ties[...].astype(BF16)

    first, final = product(dev[0], load[0]).astype(F32), product(dev[1], load[1]).astype(F32)
    pair_out[0:rows, :] = jnp.where(even, final, first).astype(BF16)
    chip_out[0:rows, :] = jnp.where(even, first, final).astype(BF16)
    pair_out[rows : rows + TIE_ROWS, :] = packed
    chip_out[rows : rows + TIE_ROWS, :] = packed


def pass_kernel(given, same):
    same[0:8, :] = given[0:8, :]


def inner_kernel(dev, load, jac, src, tgt, adm, cond, mis_hbm, mis, ends, part, sem):
    blocks, total, width = dev.shape
    edges = src.shape[1]
    src4 = jnp.concatenate([src[...]] * 4, axis=1)
    tgt4 = jnp.concatenate([tgt[...]] * 4, axis=1)
    adm4 = jnp.concatenate([adm[...]] * 4, axis=1)
    low = lax.broadcasted_iota(I32, (1, 4 * edges), 1) < 2 * edges
    hots = []
    for b in range(blocks):
        before = tgt4[b - 1 : b] if b else jnp.full((1, 4 * edges), -1, I32)
        mine = src4[b : b + 1]
        hots.append(hot_columns(jnp.where(low, *((before, mine) if b % 2 else (mine, before))), width))

    def body(here):
        scaled = [product(dev[b, here, :], load[b, here, :]) for b in range(blocks)]
        picked = [dot(scaled[b], hots[b]) for b in range(blocks)]
        previous = None
        row = []
        for b in range(blocks):
            after = picked[b + 1] if b + 1 < blocks else 0.0
            flow = adm4[b : b + 1] * (after - picked[b])
            received = 0.0 if previous is None else -previous
            flows = halves(jnp.where(low, *((received, flow) if b % 2 else (flow, received))), edges)
            previous = flow
            whole = dot(scaled[b], jac[b]) + dot_t(flows, hots[b])
            if b == 0:
                ends[0, here, :] = whole
            elif b == blocks - 1:
                ends[1, here, :] = whole
            else:
                rounded = whole.astype(BF16)
                mis[b, here, :] = rounded
                row.append((b, rounded))
            if b == blocks // 2 - 1:
                early = pl.ds(1, b)
                copy = pltpu.make_async_copy(mis.at[early, here, :], mis_hbm.at[early, here, :], sem)
                copy.start()
        sums = 0.0
        for k in range(0, len(row), 2):
            pair = row[k : k + 2]
            left = jnp.concatenate([value for _, value in pair], axis=1)
            first = pair[0][0]
            right = cond[first : first + len(pair)].reshape(len(pair) * width, cond.shape[2])
            sums = sums + dot(left, right)
        part[here, :] = sums
        copy.wait()

    row_chunks(total, 64, body)


def ends_kernel(dev, load, src, tgt, adm, cond, chip_in, pair_in, ends, part, keep, mis, out):
    blocks, total, width = dev.shape
    edges = src.shape[1]
    last = blocks - 1
    place, count = lax.axis_index("bus"), lax.axis_size("bus")
    even = place % 2 == 0
    ties = jnp.where(even, chip_in[total : total + TIE_ROWS, :].astype(F32), pair_in[total : total + TIE_ROWS, :].astype(F32))

    def twice(row):
        return jnp.concatenate([row[:, 0:edges]] * 2, axis=1)

    src_before = hot_columns(twice(ties[0:1]).astype(I32), width)
    tgt_before = hot_columns(twice(ties[1:2]).astype(I32), width)
    adm_before = twice(ties[2:3] + ties[3:4] + ties[4:5])
    adm_before = jnp.where(place == 0, 0.0, adm_before)
    src_last = hot_columns(twice(src[last : last + 1]), width)
    tgt_last = hot_columns(twice(tgt[last : last + 1]), width)
    adm_last = jnp.where(place == count - 1, 0.0, twice(adm[last : last + 1]))
    right = jnp.concatenate([cond[0], cond[last]], axis=0)
    reach = cond.shape[2]
    rate = keep[...]
    while rate.shape[0] > 1:
        half = rate.shape[0] // 2
        rate = rate[0:half] * rate[half : 2 * half]
    rate = folded(rate)
    upper = rate.astype(BF16).astype(F32)
    rate = jnp.concatenate([upper, rate - upper], axis=0)
    size = rate.shape[0]
    for k in range(0, total, 2 * size):
        out[k : k + 2 * size, reach : reach + 128] = jnp.concatenate([rate, rate], axis=0).astype(BF16)

    def body(here):
        pair_rows, chip_rows = pair_in[here, :].astype(F32), chip_in[here, :].astype(F32)
        following = jnp.where(even, pair_rows, chip_rows).astype(BF16)
        leading = jnp.where(even, chip_rows, pair_rows).astype(BF16)
        first = product(dev[0, here, :], load[0, here, :])
        flow_out = adm_last * dot(following, tgt_last)
        flow_in = adm_before * (dot(first, tgt_before) - dot(leading, src_before))
        low = (ends[0, here, :] - dot_t(halves(flow_in, edges), tgt_before)).astype(BF16)
        high = (ends[1, here, :] + dot_t(halves(flow_out, edges), src_last)).astype(BF16)
        mis[0, here, :] = low
        mis[1, here, :] = high
        sums = part[here, :] + dot(jnp.concatenate([low, high], axis=1), right)
        out[here, 0:reach] = sums.astype(BF16)

    row_chunks(total, 64, body)


def push_kernel(parts, gain, keep, states, running, rates, sent):
    count, rows, _ = parts.shape
    width = gain.shape[2]
    tiles = width // 128
    place, group = lax.axis_index("bus"), lax.axis_index("period")

    def add(k, total):
        return total + parts[k, :, 0:width].astype(F32)

    section_in = lax.fori_loop(0, count, add, jnp.zeros((rows, width), F32), unroll=8).astype(BF16)
    line = lax.broadcasted_iota(I32, (rows, width), 0)
    columns = jnp.transpose(section_in.astype(F32))
    pushed = jnp.zeros((rows, width), F32)
    for r in range(rows):
        if r < rows - SUMMED_ROWS:
            row = dot(section_in, gain[r])
        else:
            row = jnp.zeros((16, width), F32)
            for m in range(0, width, 16):
                row = row + gain[r, m : m + 16, :].astype(F32) * columns[m : m + 16, r : r + 1]
            row = jnp.sum(row, axis=0, keepdims=True)
        pushed = jnp.where(line == r, row, pushed)
    rate, state = keep[...], pushed
    shift = 1
    while shift < rows:
        reached = line >= shift
        state = state + jnp.where(reached, rate * pltpu.roll(state, shift, 0), 0.0)
        rate = rate * jnp.where(reached, pltpu.roll(rate, shift, 0), 1.0)
        shift *= 2
    states[...] = state
    running[...] = rate

    def gather(k, carried):
        after, whole = carried
        both = parts[k, :, width : width + 128].astype(F32)
        span = both[0:tiles] + both[tiles : 2 * tiles]
        rates[k] = span
        return (after * jnp.where(k > place, span, 1.0), whole * span)

    ones = jnp.ones((tiles, 128), F32)
    after, whole = lax.fori_loop(0, count, gather, (ones, ones), unroll=8)
    upper = whole.astype(BF16).astype(F32)
    share = jnp.where(place % 2 == 0, upper, whole - upper)
    last_state = folded(state[rows - 1 : rows])
    here = jnp.concatenate([last_state, share], axis=0)
    beyond = jnp.concatenate([last_state * after, share], axis=0)
    for q in range(sent.shape[0] // count):
        value = jnp.where(group == q, here, beyond).astype(BF16)
        for k in range(count):
            sent[q * count + k] = value


def enter_kernel(spans, rates, states, running, outer, inner, mis_in, out_hbm, mis, out, sems):
    blocks = mis.shape[0]
    late = pl.ds(blocks // 2, blocks - 1 - blocks // 2)
    copies = [pltpu.make_async_copy(inner.at[late], mis.at[late], sems.at[0])]
    copies += [pltpu.make_async_copy(outer.at[k], mis.at[k * (blocks - 1)], sems.at[k + 1]) for k in range(2)]
    for copy in copies:
        copy.start()
    count, tiles, _ = rates.shape
    place, group = lax.axis_index("bus"), lax.axis_index("period")

    def add(k, total):
        return total + spans[k].astype(F32)

    entering = jnp.zeros((tiles, 128), F32)
    for q in range(spans.shape[0] // count - 1):
        first = q * count
        total = lax.fori_loop(first, first + count, add, jnp.zeros((2 * tiles, 128), F32), unroll=8)[0:tiles]
        pair = (spans[first].astype(F32) + spans[first + 1].astype(F32))[tiles : 2 * tiles]
        entering = jnp.where(q < group, pair * entering + total, entering)

    def step(k, entering):
        state = spans[group * count + k].astype(F32)[0:tiles]
        return jnp.where(k < place, rates[k] * entering + state, entering)

    entering = lax.fori_loop(0, count, step, entering, unroll=8)
    out[...] = states[...] + running[...] * unfolded(entering)
    copies.append(pltpu.make_async_copy(out, out_hbm, sems.at[3]))
    copies[3].start()
    for copy in copies:
        copy.wait()


def call(kernel, shapes, inputs, cost, scratch=(), specs=None, ins=None, aliases=None):
    single = not isinstance(shapes, (list, tuple))
    return pl.pallas_call(
        kernel,
        out_shape=shapes,
        in_specs=ins or [VM] * len(inputs),
        out_specs=specs or (VM if single else [VM] * len(shapes)),
        scratch_shapes=list(scratch),
        input_output_aliases=aliases or {},
        compiler_params=PARAMS,
        cost_estimate=pl.CostEstimate(flops=int(cost * 1e9), transcendentals=0, bytes_accessed=int(cost * 3.0e6)),
    )(*inputs)


def shards(deviation, loading, jacobian, tie_source, tie_target, tie_admittance, condense, section_gain, retention):
    blocks, total, width = deviation.shape
    states_width, edges = condense.shape[2], tie_source.shape[1]
    count = lax.axis_size("bus")
    spans = count * lax.axis_size("period")
    rows = section_gain.shape[1]
    shape = jax.ShapeDtypeStruct

    payload = shape((total + TIE_ROWS, width), BF16)
    lines, weights = shape((blocks, edges), I32), shape((blocks, edges), F32)
    pair_out, chip_out, src, tgt, adm = call(
        halo_kernel,
        [payload, payload, lines, lines, weights],
        [pltpu.with_memory_space_constraint(x, pltpu.HBM) for x in (deviation, loading, tie_source, tie_target, tie_admittance)],
        0.1,
        [
            pltpu.VMEM((2, total, width), BF16),
            pltpu.VMEM((2, total, width), BF16),
            pltpu.VMEM((TIE_ROWS, width), F32),
            pltpu.SemaphoreType.DMA((7,)),
        ],
        ins=[HBM] * 5,
    )
    chip_out = call(pass_kernel, payload, (chip_out,), 10.0, aliases={0: 0})
    pairs = [(k, k ^ 1) for k in range(count)]
    groups = lax.axis_size("period")
    chips = []
    for k in range(count):
        partner = k + 1 if k % 2 else k - 1
        for g in range(groups):
            if 0 <= partner < count:
                chips.append((k * groups + g, partner * groups + g))
            else:
                chips.append((k * groups + g, k * groups + g ^ 1))
    chip_in = lax.ppermute(chip_out, ("bus", "period"), chips)
    pair_in = lax.ppermute(pair_out, "bus", pairs)
    early, inner, ends, part = call(
        inner_kernel,
        [shape((blocks, total, width), BF16), shape((blocks, total, width), BF16), shape((2, total, width), F32), shape((total, states_width), F32)],
        (deviation, loading, jacobian, src, tgt, adm, condense),
        5.0,
        [pltpu.SemaphoreType.DMA],
        [HBM, VM, VM, VM],
    )
    outer, sums = call(
        ends_kernel,
        [shape((2, total, width), BF16), shape((total, states_width + 128), BF16)],
        (deviation, loading, src, tgt, adm, condense, chip_in, pair_in, ends, part, retention[0]),
        1.0,
    )
    parts = lax.all_to_all(sums.reshape(count, rows, states_width + 128), "bus", 0, 0, tiled=True)
    tiles = 2 * states_width // 128
    states, running, rates, sent = call(
        push_kernel,
        [
            shape((rows, states_width), F32),
            shape((rows, states_width), F32),
            shape((count, tiles // 2, 128), F32),
            shape((spans, tiles, 128), BF16),
        ],
        (parts, section_gain[0], retention[0]),
        2.0,
    )
    everything = lax.all_to_all(sent, ("period", "bus"), 0, 0, tiled=True)
    out, mismatch = call(
        enter_kernel,
        [shape((rows, states_width), F32), shape((blocks, total, width), BF16)],
        (everything, rates, states, running, outer, inner, early),
        1.0,
        [pltpu.VMEM((rows, states_width), F32), pltpu.SemaphoreType.DMA((4,))],
        [HBM, HBM],
        [VM] * 6 + [HBM],
        {6: 1},
    )
    return (mismatch, out[None])


def solution(mesh):
    placed = (
        P("bus", "period", None),
        P("bus", "period", None),
        P("bus", None, None),
        P("bus", None),
        P("bus", None),
        P("bus", None),
        P("bus", None, None),
        P("period", "bus", None, None),
        P("period", "bus", None),
    )
    return jax.shard_map(
        shards,
        mesh=mesh,
        in_specs=placed,
        out_specs=(P("bus", "period", None), P("period", "bus", None)),
        check_vma=False,
    )
```
